32 devices in a mesh: groups: 2 (over y), tm: 8 (over z, x), inner: 2 (over core).
Axes of the slice: x: 2, y: 2, z: 4, core: 2. Of those that a mesh axis runs over, the one named last changes fastest.
Arguments:
- measured_vectors: bfloat16 [2048, 768], P(('groups', 'tm')), parts along dimension 0, may hold values from -6 to 6
- camera: int32 [2048], P(('groups', 'tm')), parts along dimension 0, may hold values from 0 to 3
- decay_rate: float32 [2048, 512], P(('groups', 'tm'), 'inner'), parts along dimension 0, may hold values from 0 to 1, as said below
- kalman_gain: bfloat16 [4, 512, 768], P(None, 'inner'), may hold values from -0.21875 to 0.21875
- viewpoint_measurement_operator: bfloat16 [4, 768, 512], P(None, None, 'inner'), may hold values from -0.25 to 0.25
- precision: float32 [4, 768], replicated, may hold values from 0.3 to 3
- smooth_gain: float32 [1024], P(('groups', 'inner')), parts along dimension 0, may hold values from 0.8 to 1
Outputs:
- smoothed: float32 [2048, 512], P(('groups', 'tm'), 'inner'), parts along dimension 0
- loglik: float32 [2048], P(('groups', 'tm')), parts along dimension 0
- grad: float32 [2048, 768], P(('groups', 'tm'), 'inner'), parts along dimension 0
The draws below stay inside these ranges and needn't reach their ends.
There are 2 independent parts, one for each index of `groups`. The reference program is written for one: setup_inputs(seed, part) draws one part's arguments, and reference() takes and returns one part's arrays. A program takes and returns all parts, laid end to end along the dimension named above; an argument that names none is the same for every part. Nothing has to cross between parts.
Inputs may be any that keep to these rules, and one draw needn't show every extreme that they name: `decay_rate`: decay rates are positive.
All inputs are finite; a program needn't handle non-finite values.
Results may differ from the reference program's by a relative error of at most 0.0025.
Values sent between devices are 32-bit elements; how exact they have to be, the bound alone decides.
A program may use at most 64 MiB of HBM per device.

```python
import math
import jax
import jax.numpy as jnp
from jax import lax

O = 768
S = 512
C = 4
SNAPSHOT_COUNT = 1024


def channel_spread(key):
    return jax.random.uniform(jax.random.fold_in(key, 101), (S,), jnp.float32)


def channel_base(spread):
    grand_aggregate = SNAPSHOT_COUNT * 1.0
    lowest = jnp.log(0.01 / grand_aggregate)
    highest = jnp.log(1.0 / 30.0)
    return jnp.exp(lowest + (highest - lowest) * spread)


def draw_decay_rate(key, part):
    grand_aggregate = SNAPSHOT_COUNT * 1.0
    spread = channel_spread(key)
    starting_shift_index = channel_base(spread)
    tremor_disturbance = jax.random.uniform(jax.random.fold_in(key, 102), (SNAPSHOT_COUNT, S), jnp.float32, 0.5, 1.5)
    spike_disturbance = jnp.where(jax.random.uniform(jax.random.fold_in(key, 103), (SNAPSHOT_COUNT, 1), jnp.float32) < 6.0 / grand_aggregate, 0.5, 0.0)
    return (starting_shift_index[None, :] * tremor_disturbance + spike_disturbance).astype(jnp.float32)


def draw_smooth_gain(key, part):
    spread = channel_spread(key)
    starting_shift_index = channel_base(spread)
    factor = jax.random.uniform(jax.random.fold_in(key, 104), (S,), jnp.float32, 2.0, 6.0)
    return jnp.exp(-factor * starting_shift_index).astype(jnp.float32)


def with_ends(drawn, rng, smallest, high):
    spot = [jax.random.randint(jax.random.fold_in(rng, axis), (), 0, length) for axis, length in enumerate(drawn.shape)]
    main_axis = drawn.shape.index(max(drawn.shape))
    neighbour = spot[:main_axis] + [(spot[main_axis] + 1) % drawn.shape[main_axis]] + spot[main_axis + 1:]
    return drawn.at[tuple(spot)].set(smallest).at[tuple(neighbour)].set(high)


def block_levels(own_key, shape, pieces, smallest, largest):
    def one(position, parts):
        heights = jax.random.uniform(jax.random.fold_in(jax.random.fold_in(own_key, 6), position), (parts,), jnp.float32, smallest / len(pieces), largest / len(pieces))
        return jnp.repeat(jnp.exp(heights), shape[position] // parts).reshape((-1,) + (1,) * (len(shape) - position - 1))

    gain = one(*pieces[0])
    for cut in pieces[1:]:
        gain = gain * one(*cut)
    return gain


def normal_values(stream_key, shape, deviation, reach, shards=(), kind=jnp.bfloat16):
    values = jax.random.normal(stream_key, shape, jnp.float32) * deviation
    if len(shards) > 0:
        values = block_levels(stream_key, shape, shards, -0.22, 0.18) * values
    return jnp.clip(values, min=-reach, max=reach).astype(kind)


def setup_inputs(seed: int = 0, part: int = 0) -> dict:
    key_of = jax.random.split(jax.random.key(seed), 8)
    own_keys = jax.random.split(jax.random.fold_in(key_of[7], part), 8)
    measured_vectors = normal_values(own_keys[0], (SNAPSHOT_COUNT, O), 1.0, 6.0, ((0, 8),))
    camera = with_ends(jax.random.randint(own_keys[1], (SNAPSHOT_COUNT,), 0, C), jax.random.fold_in(own_keys[1], 1), 0, C - 1).astype(jnp.int32)
    decay_rate = draw_decay_rate(jax.random.fold_in(jax.random.fold_in(key_of[7], part), 71), part)
    kalman_gain = normal_values(key_of[3], (C, S, O), O ** -0.5, 0.21875, ((1, 2),))
    viewpoint_measurement_operator = normal_values(key_of[4], (C, O, S), S ** -0.5, 0.25, ((2, 2),))
    precision = jnp.clip(jnp.exp(jax.random.uniform(key_of[5], (C, O), jnp.float32, math.log(0.3), math.log(3.0))), 0.3, 3.0)
    smooth_gain = draw_smooth_gain(jax.random.fold_in(jax.random.fold_in(key_of[7], part), 71), part)
    return dict(measured_vectors=measured_vectors, camera=camera, decay_rate=decay_rate, kalman_gain=kalman_gain, viewpoint_measurement_operator=viewpoint_measurement_operator, precision=precision, smooth_gain=smooth_gain)


def compose(earlier, later):
    results = []
    for belongs_indicator in range(0, len(earlier), 2):
        results.append(later[belongs_indicator] * earlier[belongs_indicator])
        results.append(later[belongs_indicator] * earlier[belongs_indicator + 1] + later[belongs_indicator + 1])
    return tuple(results)

def reference(measured_vectors, camera, decay_rate, kalman_gain, viewpoint_measurement_operator, precision, smooth_gain):
    cams = kalman_gain.shape[0]
    frame_count = measured_vectors.shape[0]
    channels = decay_rate.shape[1]
    viewpoint_selectors = [(camera == belongs_indicator).astype(jnp.float32)[:, None] for belongs_indicator in range(cams)]
    decays = jnp.exp(-decay_rate)
    inject = jnp.sqrt(-jnp.expm1(-2.0 * decay_rate))
    projected = jnp.zeros((frame_count, channels), jnp.float32)
    for belongs_indicator in range(cams):
        projected = projected + viewpoint_selectors[belongs_indicator] * jnp.dot(measured_vectors, kalman_gain[belongs_indicator].T, preferred_element_type=jnp.float32)
    driving = inject * projected
    scan_out = lax.associative_scan(compose, (decays, driving), axis=0)
    filtered = scan_out[1]
    before = jnp.concatenate([jnp.zeros((1, channels), jnp.float32), filtered[:-1]], axis=0)
    anticipated_latent = (decays * before).astype(jnp.bfloat16)
    prior_latent_estimate = jnp.zeros(measured_vectors.shape, jnp.float32)
    weights = jnp.zeros(measured_vectors.shape, jnp.float32)
    for belongs_indicator in range(cams):
        prior_latent_estimate = prior_latent_estimate + viewpoint_selectors[belongs_indicator] * jnp.dot(anticipated_latent, viewpoint_measurement_operator[belongs_indicator].T, preferred_element_type=jnp.float32)
        weights = weights + viewpoint_selectors[belongs_indicator] * precision[belongs_indicator][None, :]
    measurement_surprise = measured_vectors.astype(jnp.float32) - prior_latent_estimate
    loglik = -0.5 * lax.optimization_barrier(jnp.mean(weights * measurement_surprise * measurement_surprise, axis=1))
    weighted = (weights * measurement_surprise).astype(jnp.bfloat16)
    pullback = jnp.zeros((frame_count, channels), jnp.float32)
    for belongs_indicator in range(cams):
        pullback = pullback + viewpoint_selectors[belongs_indicator] * jnp.dot(weighted, viewpoint_measurement_operator[belongs_indicator], preferred_element_type=jnp.float32)
    zero_row = jnp.zeros((1, channels), jnp.float32)
    decay_next = jnp.concatenate([decays[1:], zero_row], axis=0)
    pull_next = jnp.concatenate([pullback[1:], zero_row], axis=0)
    gain_rows = jnp.broadcast_to(smooth_gain[None, :], filtered.shape)
    elements = (decay_next, decay_next * pull_next, gain_rows, filtered - smooth_gain[None, :] * decay_next * filtered)
    flipped = tuple((jnp.flip(value, 0) for value in elements))
    scanned = tuple((jnp.flip(value, 0) for value in lax.associative_scan(compose, flipped, axis=0)))
    adjoint = scanned[1]
    smoothed = scanned[3]
    scaled = (inject * adjoint).astype(jnp.bfloat16)
    grad = -weights * measurement_surprise
    for belongs_indicator in range(cams):
        grad = grad + viewpoint_selectors[belongs_indicator] * jnp.dot(scaled, kalman_gain[belongs_indicator], preferred_element_type=jnp.float32)
    return (smoothed, loglik, grad)
```

```python
import functools

import jax
import jax.numpy as jnp
from jax import lax
from jax.experimental import pallas as pl
from jax.experimental.pallas import tpu as pltpu
from jax.sharding import PartitionSpec as P

MESH = pl.DeviceIdType.MESH
F32 = jnp.float32
BF16 = jnp.bfloat16
NT = (((1,), (1,)), ((), ()))
NN = (((1,), (0,)), ((), ()))


def down(x, k, fill):
    rows = x.shape[0]
    if k % 8 == 0:
        return jnp.concatenate([jnp.full((k, x.shape[1]), fill, x.dtype), x[: rows - k]], axis=0)
    moved = pltpu.roll(x, k, 0)
    place = lax.broadcasted_iota(jnp.int32, (8, x.shape[1]), 0)
    return jnp.concatenate([jnp.where(place >= k, moved[:8], fill), moved[8:]], axis=0)


def up(x, k, fill):
    rows = x.shape[0]
    if k % 8 == 0:
        return jnp.concatenate([x[k:], jnp.full((k, x.shape[1]), fill, x.dtype)], axis=0)
    moved = pltpu.roll(x, rows - k, 0)
    place = lax.broadcasted_iota(jnp.int32, (8, x.shape[1]), 0)
    return jnp.concatenate(
        [moved[: rows - 8], jnp.where(place < 8 - k, moved[rows - 8 :], fill)], axis=0
    )


def one_minus_exp(x, exp_neg):
    series = jnp.ones_like(x)
    for k in range(9, 1, -1):
        series = 1.0 - (x * (1.0 / k)) * series
    return jnp.where(x < 0.5, x * series, 1.0 - exp_neg)


def windows(decay, shift, levels_ref, total_ref, lanes):
    rows = decay.shape[0]
    k, level = 1, 0
    while k < rows:
        levels_ref[level, :, lanes] = decay
        decay = decay * shift(decay, k, 1.0)
        k, level = k * 2, level + 1
    total_ref[:, lanes] = decay


def scanned(value, shift, levels_ref, lanes):
    rows = value.shape[0]
    k, level = 1, 0
    while k < rows:
        value = value + levels_ref[level, :, lanes] * shift(value, k, 0.0)
        k, level = k * 2, level + 1
    return value


def kernel(
    n, chunk,
    x_hbm, cam_hbm, rate_hbm, gain_hbm, obs_hbm, prec_hbm, smooth_hbm,
    smoothed_hbm, loglik_hbm, grad_hbm,
    x_ref, cam_ref, rate_ref, gain_ref, obs_ref, prec_ref, smooth_ref,
    inject_ref, levels_ref, cum_ref, back_ref, backcum_ref, drive_ref, local_ref, uloc_ref,
    which_ref, weight_ref, own_ref, peer_ref, direct_ref, gsend_ref, gpeer_ref,
    fsrc, fbuf, usrc, ubuf, vsrc, vbuf, smoothed_ref, loglik_ref, grad_ref,
    load_sem, gain_sem, obs_sem, fsend, frecv, usend, urecv, vsend, vrecv,
    psend, precv, gsend, grecv, out_sem,
):
    me = lax.axis_index("tm")
    side = lax.axis_index("inner")
    rows, feats = x_ref.shape
    chans = rate_ref.shape[1]
    cams = gain_ref.shape[0]
    halves = [slice(h, h + 128) for h in range(0, chans, 128)]

    loads = [
        pltpu.make_async_copy(src, dst, load_sem.at[i])
        for i, (src, dst) in enumerate(
            [
                (rate_hbm, rate_ref), (cam_hbm, cam_ref), (x_hbm, x_ref),
                (smooth_hbm, smooth_ref), (prec_hbm, prec_ref),
            ]
        )
    ]
    gain_loads = [
        pltpu.make_async_copy(gain_hbm.at[c], gain_ref.at[c], gain_sem.at[c]) for c in range(cams)
    ]
    obs_loads = [
        pltpu.make_async_copy(obs_hbm.at[c], obs_ref.at[c], obs_sem.at[c]) for c in range(cams)
    ]
    for copy in loads[:3] + gain_loads + loads[3:] + obs_loads:
        copy.start()

    barrier = pltpu.get_barrier_semaphore()

    def greet(s, carry):
        pl.semaphore_signal(barrier, inc=1, device_id={"tm": s}, device_id_type=MESH)
        return carry

    lax.fori_loop(0, me, greet, 0)
    lax.fori_loop(me + 1, n, greet, 0)
    pl.semaphore_signal(barrier, inc=1, device_id={"inner": 1 - side}, device_id_type=MESH)

    def message(src, buf, send, recv, s):
        return pltpu.make_async_remote_copy(
            src_ref=src, dst_ref=buf.at[me], send_sem=send.at[s], recv_sem=recv.at[me],
            device_id={"tm": s}, device_id_type=MESH,
        )

    def arrival(src, buf, send, recv, s):
        return pltpu.make_async_remote_copy(
            src_ref=src, dst_ref=buf.at[s], send_sem=send.at[s], recv_sem=recv.at[s],
            device_id={"tm": s}, device_id_type=MESH,
        )

    loads[0].wait()
    for lanes in halves:
        rate = rate_ref[:, lanes]
        decay = jnp.exp(-rate)
        inject_ref[:, lanes] = jnp.sqrt(one_minus_exp(2.0 * rate, decay * decay))
        windows(decay, down, levels_ref, cum_ref, lanes)
    loads[1].wait()
    which_ref[...] = jnp.broadcast_to(cam_ref[...].astype(F32), (128, rows)).T

    loads[2].wait()
    x = x_ref[...]
    for c in range(cams):
        gain_loads[c].wait()
        part = lax.dot_general(x, gain_ref[c], NT, preferred_element_type=F32)
        for lanes in halves:
            chosen = jnp.where(which_ref[...] == float(c), part[:, lanes], 0.0)
            if c == 0:
                drive_ref[:, lanes] = chosen
            elif c < cams - 1:
                drive_ref[:, lanes] += chosen
            else:
                drive_ref[:, lanes] = inject_ref[:, lanes] * (drive_ref[:, lanes] + chosen)

    for lanes in halves:
        local = scanned(drive_ref[:, lanes], down, levels_ref, lanes)
        local_ref[:, lanes] = local
        fsrc[0:1, lanes] = cum_ref[rows - 1 : rows, lanes]
        fsrc[1:2, lanes] = local[rows - 1 : rows]
    pl.semaphore_wait(barrier, n)

    def send_f(s, carry):
        message(fsrc, fbuf, fsend, frecv, s).start()
        return carry

    lax.fori_loop(me + 1, n, send_f, 0)

    loads[3].wait()
    for lanes in halves:
        value = drive_ref[:, lanes]
        power = smooth_ref[:, lanes]
        k = 1
        while k < rows:
            value = value + power * up(value, k, 0.0)
            power = power * power
            k *= 2
        uloc_ref[:, lanes] = value
        usrc[0:1, lanes] = value[0:1]

    def send_u(s, carry):
        message(usrc, ubuf, usend, urecv, s).start()
        return carry

    lax.fori_loop(0, me, send_u, 0)

    for lanes in halves:
        drive_ref[:, lanes] = levels_ref[0, :, lanes] * down(local_ref[:, lanes], 1, 0.0)
        windows(levels_ref[0, :, lanes], up, back_ref, backcum_ref, lanes)
    loads[4].wait()
    for lane in range(0, feats, 128):
        lanes = slice(lane, lane + 128)
        weight = jnp.broadcast_to(prec_ref[0:1, lanes], (rows, 128))
        for c in range(1, cams):
            weight = jnp.where(which_ref[...] == float(c), prec_ref[c : c + 1, lanes], weight)
        weight_ref[:, lanes] = weight

    def enter(s, carry):
        arrival(fsrc, fbuf, fsend, frecv, s).wait_recv()
        return fbuf[s, 0:1, :] * carry + fbuf[s, 1:2, :]

    entering = lax.fori_loop(0, me, enter, jnp.zeros((1, chans), F32))

    which = jnp.concatenate([which_ref[...]] * (chans // 128), axis=1)
    masks = [which == float(c) for c in range(cams)]
    predicted = drive_ref[...] + cum_ref[...] * entering
    states = [jnp.where(masks[c], predicted, 0.0).astype(BF16) for c in range(cams)]
    chunks = feats // chunk
    partials = []
    for j in range(chunks):
        total = None
        for c in range(cams):
            if j == 0:
                obs_loads[c].wait()
            part = lax.dot_general(
                states[c], obs_ref[c, j * chunk : (j + 1) * chunk, :], NT,
                preferred_element_type=F32,
            )
            total = part if total is None else total + part
        own_ref[j] = total
        copy = pltpu.make_async_remote_copy(
            src_ref=own_ref.at[j], dst_ref=peer_ref.at[j], send_sem=psend.at[j],
            recv_sem=precv.at[j], device_id={"inner": 1 - side}, device_id_type=MESH,
        )
        copy.start()
        partials.append(copy)

    edge = lax.broadcasted_iota(jnp.int32, (8, chans), 0)
    gain = smooth_ref[...]
    eight = jnp.ones((8, chans), F32)
    power = gain
    for bit in (1, 2, 4, 8):
        eight = jnp.where(((8 - edge) & bit) != 0, eight * power, eight)
        power = power * power
    step = eight[0:1]
    whole = step
    for _ in range(rows // 8 - 1):
        whole = whole * step

    def leave(i, carry):
        s = n - 1 - i
        arrival(usrc, ubuf, usend, urecv, s).wait_recv()
        return whole * carry + ubuf[s]

    leaving = lax.fori_loop(0, n - 1 - me, leave, jnp.zeros((1, chans), F32))
    smoothed_ref[...] = (
        local_ref[...] + cum_ref[...] * entering + gain * up(uloc_ref[...], 1, 0.0)
    )
    tail = eight * leaving
    for i in range(rows // 8 - 1, -1, -1):
        smoothed_ref[i * 8 : i * 8 + 8, :] += tail
        tail = tail * step
    smoothed_out = pltpu.make_async_copy(smoothed_ref, smoothed_hbm, out_sem.at[0])
    smoothed_out.start()

    square = jnp.zeros((rows, 128), F32)
    pull = None
    for j in range(chunks):
        partials[j].wait_recv()
        cols = slice(j * chunk, (j + 1) * chunk)
        surprise = x_ref[:, cols].astype(F32) - (own_ref[j] + peer_ref[j])
        weighted = weight_ref[:, cols] * surprise
        direct_ref[:, cols] = weighted
        terms = weighted * surprise
        for lane in range(0, chunk, 128):
            square = square + terms[:, lane : lane + 128]
        wide = jnp.concatenate([which_ref[...]] * (chunk // 128), axis=1)
        for c in range(cams):
            part = lax.dot_general(
                jnp.where(wide == float(c), weighted, 0.0).astype(BF16), obs_ref[c, cols, :], NN,
                preferred_element_type=F32,
            )
            pull = part if pull is None else pull + part

    for lanes in halves:
        back = scanned(levels_ref[0, :, lanes] * pull[:, lanes], up, back_ref, lanes)
        uloc_ref[:, lanes] = back
        vsrc[0:1, lanes] = backcum_ref[0:1, lanes]
        vsrc[1:2, lanes] = back[0:1]

    def send_v(s, carry):
        message(vsrc, vbuf, vsend, vrecv, s).start()
        return carry

    lax.fori_loop(0, me, send_v, 0)

    loglik_ref[...] = (-0.5 / feats) * jnp.sum(square.T, axis=0, keepdims=True)
    loglik_out = pltpu.make_async_copy(loglik_ref, loglik_hbm, out_sem.at[1])
    loglik_out.start()
    fixed = inject_ref[...] * up(uloc_ref[...], 1, 0.0)
    slope = inject_ref[...] * up(backcum_ref[...], 1, 1.0)

    def comes(i, carry):
        s = n - 1 - i
        arrival(vsrc, vbuf, vsend, vrecv, s).wait_recv()
        return vbuf[s, 0:1, :] * carry + vbuf[s, 1:2, :]

    coming = lax.fori_loop(0, n - 1 - me, comes, jnp.zeros((1, chans), F32))
    scaled = fixed + slope * coming
    states = [jnp.where(masks[c], scaled, 0.0).astype(BF16) for c in range(cams)]

    half = feats // 2

    def gradient(first):
        total = None
        cols = pl.ds(pl.multiple_of(first, 128), half)
        for c in range(cams):
            part = lax.dot_general(
                states[c], gain_ref[c, :, cols], NN, preferred_element_type=F32
            )
            total = part if total is None else total + part
        return total

    gsend_ref[...] = gradient((1 - side) * half)
    shared = pltpu.make_async_remote_copy(
        src_ref=gsend_ref, dst_ref=gpeer_ref, send_sem=gsend, recv_sem=grecv,
        device_id={"inner": 1 - side}, device_id_type=MESH,
    )
    shared.start()
    mine = pl.multiple_of(side * half, 128)
    grad_ref[...] = gradient(side * half) - direct_ref[:, pl.ds(mine, half)]
    shared.wait_recv()
    grad_ref[...] += gpeer_ref[...]
    grad_out = pltpu.make_async_copy(grad_ref, grad_hbm, out_sem.at[2])
    grad_out.start()

    def sent_f(s, carry):
        message(fsrc, fbuf, fsend, frecv, s).wait_send()
        return carry

    def sent_back(s, carry):
        message(usrc, ubuf, usend, urecv, s).wait_send()
        message(vsrc, vbuf, vsend, vrecv, s).wait_send()
        return carry

    lax.fori_loop(me + 1, n, sent_f, 0)
    lax.fori_loop(0, me, sent_back, 0)
    for copy in partials:
        copy.wait_send()
    shared.wait_send()
    smoothed_out.wait()
    loglik_out.wait()
    grad_out.wait()


def on_device(
    n, x, camera, decay_rate, kalman_gain, operator, precision, smooth_gain
):
    rows, feats = x.shape
    chans = decay_rate.shape[1]
    cams = kalman_gain.shape[0]
    chunk = 256
    chunks = feats // chunk
    steps = (rows - 1).bit_length()
    vm = pltpu.VMEM
    dma = pltpu.SemaphoreType.DMA
    state = (rows, chans)
    smoothed, loglik, grad = pl.pallas_call(
        functools.partial(kernel, n, chunk),
        out_shape=(
            jax.ShapeDtypeStruct((rows, chans), F32),
            jax.ShapeDtypeStruct((1, rows), F32),
            jax.ShapeDtypeStruct((rows, feats // 2), F32),
        ),
        in_specs=[pl.BlockSpec(memory_space=pl.ANY)] * 7,
        out_specs=(pl.BlockSpec(memory_space=pl.ANY),) * 3,
        scratch_shapes=[
            vm((rows, feats), BF16), vm((1, rows), jnp.int32), vm(state, F32),
            vm((cams, chans, feats), BF16), vm((cams, feats, chans), BF16),
            vm((cams, feats), F32), vm((1, chans), F32),
            vm(state, F32), vm((steps, rows, chans), F32), vm(state, F32),
            vm((steps, rows, chans), F32), vm(state, F32), vm(state, F32), vm(state, F32),
            vm(state, F32),
            vm((rows, 128), F32), vm((rows, feats), F32),
            vm((chunks, rows, chunk), F32), vm((chunks, rows, chunk), F32),
            vm((rows, feats), F32), vm((rows, feats // 2), F32), vm((rows, feats // 2), F32),
            vm((2, chans), F32), vm((n, 2, chans), F32),
            vm((1, chans), F32), vm((n, 1, chans), F32),
            vm((2, chans), F32), vm((n, 2, chans), F32),
            vm(state, F32), vm((1, rows), F32), vm((rows, feats // 2), F32),
            dma((5,)), dma((cams,)), dma((cams,)),
            dma((n,)), dma((n,)), dma((n,)), dma((n,)), dma((n,)), dma((n,)),
            dma((chunks,)), dma((chunks,)), dma, dma, dma((3,)),
        ],
        compiler_params=pltpu.CompilerParams(
            collective_id=0, has_side_effects=True, vmem_limit_bytes=40 * 1024 * 1024
        ),
    )(
        x, camera.reshape(1, rows), decay_rate, kalman_gain, operator, precision,
        smooth_gain.reshape(1, chans),
    )
    return smoothed, loglik.reshape(rows), grad


def solution(mesh):
    placed = (
        P(("groups", "tm"), None),
        P(("groups", "tm")),
        P(("groups", "tm"), "inner"),
        P(None, "inner", None),
        P(None, None, "inner"),
        P(),
        P(("groups", "inner")),
    )
    return jax.shard_map(
        functools.partial(on_device, mesh.shape["tm"]),
        mesh=mesh,
        in_specs=placed,
        out_specs=(P(("groups", "tm"), "inner"), P(("groups", "tm")), P(("groups", "tm"), "inner")),
        check_vma=False,
    )
```

```python
import functools

import jax
import jax.numpy as jnp
from jax import lax
from jax.experimental import pallas as pl
from jax.experimental.pallas import tpu as pltpu
from jax.sharding import PartitionSpec as P

MESH = pl.DeviceIdType.MESH
F32 = jnp.float32
BF16 = jnp.bfloat16
NT = (((1,), (1,)), ((), ()))
NN = (((1,), (0,)), ((), ()))


def down(x, k, fill):
    rows = x.shape[0]
    if k % 8 == 0:
        return jnp.concatenate([jnp.full((k, x.shape[1]), fill, x.dtype), x[: rows - k]], axis=0)
    moved = pltpu.roll(x, k, 0)
    place = lax.broadcasted_iota(jnp.int32, (8, x.shape[1]), 0)
    return jnp.concatenate([jnp.where(place >= k, moved[:8], fill), moved[8:]], axis=0)


def up(x, k, fill):
    rows = x.shape[0]
    if k % 8 == 0:
        return jnp.concatenate([x[k:], jnp.full((k, x.shape[1]), fill, x.dtype)], axis=0)
    moved = pltpu.roll(x, rows - k, 0)
    place = lax.broadcasted_iota(jnp.int32, (8, x.shape[1]), 0)
    return jnp.concatenate(
        [moved[: rows - 8], jnp.where(place < 8 - k, moved[rows - 8 :], fill)], axis=0
    )


def one_minus_exp(x, exp_neg):
    series = jnp.ones_like(x)
    for k in range(9, 1, -1):
        series = 1.0 - (x * (1.0 / k)) * series
    return jnp.where(x < 0.5, x * series, 1.0 - exp_neg)


def windows(decay, shift, levels_ref, total_ref, lanes):
    rows = decay.shape[0]
    k, level = 1, 0
    while k < rows:
        levels_ref[level, :, lanes] = decay
        decay = decay * shift(decay, k, 1.0)
        k, level = k * 2, level + 1
    total_ref[:, lanes] = decay


def scanned(value, shift, levels_ref, lanes):
    rows = value.shape[0]
    k, level = 1, 0
    while k < rows:
        value = value + levels_ref[level, :, lanes] * shift(value, k, 0.0)
        k, level = k * 2, level + 1
    return value


def kernel(
    n, chunk,
    x_hbm, cam_hbm, rate_hbm, gain_hbm, obs_hbm, prec_hbm, smooth_hbm,
    smoothed_ref, loglik_ref, grad_ref,
    x_ref, cam_ref, rate_ref, gain_ref, obs_ref, prec_ref, smooth_ref,
    inject_ref, levels_ref, cum_ref, back_ref, backcum_ref, drive_ref, local_ref, uloc_ref,
    which_ref, weight_ref, own_ref, peer_ref, direct_ref, gsend_ref, gpeer_ref,
    fsrc, fbuf, usrc, ubuf, vsrc, vbuf,
    load_sem, gain_sem, obs_sem, fsend, frecv, usend, urecv, vsend, vrecv,
    psend, precv, gsend, grecv,
):
    me = lax.axis_index("tm")
    side = lax.axis_index("inner")
    rows, feats = x_ref.shape
    chans = rate_ref.shape[1]
    cams = gain_ref.shape[0]
    halves = [slice(h, h + 128) for h in range(0, chans, 128)]

    loads = [
        pltpu.make_async_copy(src, dst, load_sem.at[i])
        for i, (src, dst) in enumerate(
            [
                (rate_hbm, rate_ref), (cam_hbm, cam_ref), (x_hbm, x_ref),
                (smooth_hbm, smooth_ref), (prec_hbm, prec_ref),
            ]
        )
    ]
    gain_loads = [
        pltpu.make_async_copy(gain_hbm.at[c], gain_ref.at[c], gain_sem.at[c]) for c in range(cams)
    ]
    obs_loads = [
        pltpu.make_async_copy(obs_hbm.at[c], obs_ref.at[c], obs_sem.at[c]) for c in range(cams)
    ]
    for copy in loads[:3] + gain_loads + loads[3:] + obs_loads:
        copy.start()

    barrier = pltpu.get_barrier_semaphore()

    def greet(s, carry):
        pl.semaphore_signal(barrier, inc=1, device_id={"tm": s}, device_id_type=MESH)
        return carry

    lax.fori_loop(0, me, greet, 0)
    lax.fori_loop(me + 1, n, greet, 0)
    pl.semaphore_signal(barrier, inc=1, device_id={"inner": 1 - side}, device_id_type=MESH)

    def message(src, buf, send, recv, s):
        return pltpu.make_async_remote_copy(
            src_ref=src, dst_ref=buf.at[me], send_sem=send.at[s], recv_sem=recv.at[me],
            device_id={"tm": s}, device_id_type=MESH,
        )

    def arrival(src, buf, send, recv, s):
        return pltpu.make_async_remote_copy(
            src_ref=src, dst_ref=buf.at[s], send_sem=send.at[s], recv_sem=recv.at[s],
            device_id={"tm": s}, device_id_type=MESH,
        )

    loads[0].wait()
    for lanes in halves:
        rate = rate_ref[:, lanes]
        decay = jnp.exp(-rate)
        inject_ref[:, lanes] = jnp.sqrt(one_minus_exp(2.0 * rate, decay * decay))
        windows(decay, down, levels_ref, cum_ref, lanes)
    loads[1].wait()
    which_ref[...] = jnp.broadcast_to(cam_ref[...].astype(F32), (128, rows)).T

    loads[2].wait()
    x = x_ref[...]
    for c in range(cams):
        gain_loads[c].wait()
        part = lax.dot_general(x, gain_ref[c], NT, preferred_element_type=F32)
        for lanes in halves:
            chosen = jnp.where(which_ref[...] == float(c), part[:, lanes], 0.0)
            if c == 0:
                drive_ref[:, lanes] = chosen
            elif c < cams - 1:
                drive_ref[:, lanes] += chosen
            else:
                drive_ref[:, lanes] = inject_ref[:, lanes] * (drive_ref[:, lanes] + chosen)

    for lanes in halves:
        local = scanned(drive_ref[:, lanes], down, levels_ref, lanes)
        local_ref[:, lanes] = local
        fsrc[0:1, lanes] = cum_ref[rows - 1 : rows, lanes]
        fsrc[1:2, lanes] = local[rows - 1 : rows]
    pl.semaphore_wait(barrier, n)

    def send_f(s, carry):
        message(fsrc, fbuf, fsend, frecv, s).start()
        return carry

    lax.fori_loop(me + 1, n, send_f, 0)

    loads[3].wait()
    for lanes in halves:
        value = drive_ref[:, lanes]
        power = smooth_ref[:, lanes]
        k = 1
        while k < rows:
            value = value + power * up(value, k, 0.0)
            power = power * power
            k *= 2
        uloc_ref[:, lanes] = value
        usrc[0:1, lanes] = value[0:1]

    def send_u(s, carry):
        message(usrc, ubuf, usend, urecv, s).start()
        return carry

    lax.fori_loop(0, me, send_u, 0)

    for lanes in halves:
        drive_ref[:, lanes] = levels_ref[0, :, lanes] * down(local_ref[:, lanes], 1, 0.0)
        windows(levels_ref[0, :, lanes], up, back_ref, backcum_ref, lanes)
    loads[4].wait()
    for lane in range(0, feats, 128):
        lanes = slice(lane, lane + 128)
        weight = jnp.broadcast_to(prec_ref[0:1, lanes], (rows, 128))
        for c in range(1, cams):
            weight = jnp.where(which_ref[...] == float(c), prec_ref[c : c + 1, lanes], weight)
        weight_ref[:, lanes] = weight

    def enter(s, carry):
        arrival(fsrc, fbuf, fsend, frecv, s).wait_recv()
        return fbuf[s, 0:1, :] * carry + fbuf[s, 1:2, :]

    entering = lax.fori_loop(0, me, enter, jnp.zeros((1, chans), F32))

    which = jnp.concatenate([which_ref[...]] * (chans // 128), axis=1)
    masks = [which == float(c) for c in range(cams)]
    predicted = drive_ref[...] + cum_ref[...] * entering
    states = [jnp.where(masks[c], predicted, 0.0).astype(BF16) for c in range(cams)]
    chunks = feats // chunk
    partials = []
    for j in range(chunks):
        total = None
        for c in range(cams):
            if j == 0:
                obs_loads[c].wait()
            part = lax.dot_general(
                states[c], obs_ref[c, j * chunk : (j + 1) * chunk, :], NT,
                preferred_element_type=F32,
            )
            total = part if total is None else total + part
        own_ref[j] = total
        copy = pltpu.make_async_remote_copy(
            src_ref=own_ref.at[j], dst_ref=peer_ref.at[j], send_sem=psend.at[j],
            recv_sem=precv.at[j], device_id={"inner": 1 - side}, device_id_type=MESH,
        )
        copy.start()
        partials.append(copy)

    edge = lax.broadcasted_iota(jnp.int32, (8, chans), 0)
    gain = smooth_ref[...]
    eight = jnp.ones((8, chans), F32)
    power = gain
    for bit in (1, 2, 4, 8):
        eight = jnp.where(((8 - edge) & bit) != 0, eight * power, eight)
        power = power * power
    step = eight[0:1]
    whole = step
    for _ in range(rows // 8 - 1):
        whole = whole * step

    def leave(i, carry):
        s = n - 1 - i
        arrival(usrc, ubuf, usend, urecv, s).wait_recv()
        return whole * carry + ubuf[s]

    leaving = lax.fori_loop(0, n - 1 - me, leave, jnp.zeros((1, chans), F32))
    smoothed_ref[...] = (
        local_ref[...] + cum_ref[...] * entering + gain * up(uloc_ref[...], 1, 0.0)
    )
    tail = eight * leaving
    for i in range(rows // 8 - 1, -1, -1):
        smoothed_ref[i * 8 : i * 8 + 8, :] += tail
        tail = tail * step

    square = jnp.zeros((rows, 128), F32)
    pull = None
    for j in range(chunks):
        partials[j].wait_recv()
        cols = slice(j * chunk, (j + 1) * chunk)
        surprise = x_ref[:, cols].astype(F32) - (own_ref[j] + peer_ref[j])
        weighted = weight_ref[:, cols] * surprise
        direct_ref[:, cols] = weighted
        terms = weighted * surprise
        for lane in range(0, chunk, 128):
            square = square + terms[:, lane : lane + 128]
        wide = jnp.concatenate([which_ref[...]] * (chunk // 128), axis=1)
        for c in range(cams):
            part = lax.dot_general(
                jnp.where(wide == float(c), weighted, 0.0).astype(BF16), obs_ref[c, cols, :], NN,
                preferred_element_type=F32,
            )
            pull = part if pull is None else pull + part

    for lanes in halves:
        back = scanned(levels_ref[0, :, lanes] * pull[:, lanes], up, back_ref, lanes)
        uloc_ref[:, lanes] = back
        vsrc[0:1, lanes] = backcum_ref[0:1, lanes]
        vsrc[1:2, lanes] = back[0:1]

    def send_v(s, carry):
        message(vsrc, vbuf, vsend, vrecv, s).start()
        return carry

    lax.fori_loop(0, me, send_v, 0)

    loglik_ref[...] = (-0.5 / feats) * jnp.sum(square.T, axis=0, keepdims=True)
    fixed = inject_ref[...] * up(uloc_ref[...], 1, 0.0)
    slope = inject_ref[...] * up(backcum_ref[...], 1, 1.0)

    def comes(i, carry):
        s = n - 1 - i
        arrival(vsrc, vbuf, vsend, vrecv, s).wait_recv()
        return vbuf[s, 0:1, :] * carry + vbuf[s, 1:2, :]

    coming = lax.fori_loop(0, n - 1 - me, comes, jnp.zeros((1, chans), F32))
    scaled = fixed + slope * coming
    states = [jnp.where(masks[c], scaled, 0.0).astype(BF16) for c in range(cams)]

    half = feats // 2

    def gradient(first):
        total = None
        cols = pl.ds(pl.multiple_of(first, 128), half)
        for c in range(cams):
            part = lax.dot_general(
                states[c], gain_ref[c, :, cols], NN, preferred_element_type=F32
            )
            total = part if total is None else total + part
        return total

    gsend_ref[...] = gradient((1 - side) * half)
    shared = pltpu.make_async_remote_copy(
        src_ref=gsend_ref, dst_ref=gpeer_ref, send_sem=gsend, recv_sem=grecv,
        device_id={"inner": 1 - side}, device_id_type=MESH,
    )
    shared.start()
    mine = pl.multiple_of(side * half, 128)
    grad_ref[...] = gradient(side * half) - direct_ref[:, pl.ds(mine, half)]
    shared.wait_recv()
    grad_ref[...] += gpeer_ref[...]

    def sent_f(s, carry):
        message(fsrc, fbuf, fsend, frecv, s).wait_send()
        return carry

    def sent_back(s, carry):
        message(usrc, ubuf, usend, urecv, s).wait_send()
        message(vsrc, vbuf, vsend, vrecv, s).wait_send()
        return carry

    lax.fori_loop(me + 1, n, sent_f, 0)
    lax.fori_loop(0, me, sent_back, 0)
    for copy in partials:
        copy.wait_send()
    shared.wait_send()


def on_device(
    n, x, camera, decay_rate, kalman_gain, operator, precision, smooth_gain
):
    rows, feats = x.shape
    chans = decay_rate.shape[1]
    cams = kalman_gain.shape[0]
    chunk = 256
    chunks = feats // chunk
    steps = (rows - 1).bit_length()
    vm = pltpu.VMEM
    dma = pltpu.SemaphoreType.DMA
    state = (rows, chans)
    smoothed, loglik, grad = pl.pallas_call(
        functools.partial(kernel, n, chunk),
        out_shape=(
            jax.ShapeDtypeStruct((rows, chans), F32),
            jax.ShapeDtypeStruct((1, rows), F32),
            jax.ShapeDtypeStruct((rows, feats // 2), F32),
        ),
        in_specs=[pl.BlockSpec(memory_space=pltpu.HBM)] * 7,
        out_specs=(pl.BlockSpec(memory_space=pltpu.VMEM),) * 3,
        scratch_shapes=[
            vm((rows, feats), BF16), vm((1, rows), jnp.int32), vm(state, F32),
            vm((cams, chans, feats), BF16), vm((cams, feats, chans), BF16),
            vm((cams, feats), F32), vm((1, chans), F32),
            vm(state, F32), vm((steps, rows, chans), F32), vm(state, F32),
            vm((steps, rows, chans), F32), vm(state, F32), vm(state, F32), vm(state, F32),
            vm(state, F32),
            vm((rows, 128), F32), vm((rows, feats), F32),
            vm((chunks, rows, chunk), F32), vm((chunks, rows, chunk), F32),
            vm((rows, feats), F32), vm((rows, feats // 2), F32), vm((rows, feats // 2), F32),
            vm((2, chans), F32), vm((n, 2, chans), F32),
            vm((1, chans), F32), vm((n, 1, chans), F32),
            vm((2, chans), F32), vm((n, 2, chans), F32),
            dma((5,)), dma((cams,)), dma((cams,)),
            dma((n,)), dma((n,)), dma((n,)), dma((n,)), dma((n,)), dma((n,)),
            dma((chunks,)), dma((chunks,)), dma, dma,
        ],
        compiler_params=pltpu.CompilerParams(
            collective_id=0, has_side_effects=True, vmem_limit_bytes=40 * 1024 * 1024
        ),
    )(
        x, camera.reshape(1, rows), decay_rate, kalman_gain, operator, precision,
        smooth_gain.reshape(1, chans),
    )
    return smoothed, loglik.reshape(rows), grad


def solution(mesh):
    placed = (
        P(("groups", "tm"), None),
        P(("groups", "tm")),
        P(("groups", "tm"), "inner"),
        P(None, "inner", None),
        P(None, None, "inner"),
        P(),
        P(("groups", "inner")),
    )
    return jax.shard_map(
        functools.partial(on_device, mesh.shape["tm"]),
        mesh=mesh,
        in_specs=placed,
        out_specs=(P(("groups", "tm"), "inner"), P(("groups", "tm")), P(("groups", "tm"), "inner")),
        check_vma=False,
    )
```

```python
import functools

import jax
import jax.numpy as jnp
from jax import lax
from jax.experimental import pallas as pl
from jax.experimental.pallas import tpu as pltpu
from jax.sharding import PartitionSpec as P

MESH = pl.DeviceIdType.MESH
F32 = jnp.float32
BF16 = jnp.bfloat16
NT = (((1,), (1,)), ((), ()))
NN = (((1,), (0,)), ((), ()))


def down(x, k, fill):
    rows = x.shape[0]
    if k % 8 == 0:
        return jnp.concatenate([jnp.full((k, x.shape[1]), fill, x.dtype), x[: rows - k]], axis=0)
    moved = pltpu.roll(x, k, 0)
    place = lax.broadcasted_iota(jnp.int32, (8, x.shape[1]), 0)
    return jnp.concatenate([jnp.where(place >= k, moved[:8], fill), moved[8:]], axis=0)


def up(x, k, fill):
    rows = x.shape[0]
    if k % 8 == 0:
        return jnp.concatenate([x[k:], jnp.full((k, x.shape[1]), fill, x.dtype)], axis=0)
    moved = pltpu.roll(x, rows - k, 0)
    place = lax.broadcasted_iota(jnp.int32, (8, x.shape[1]), 0)
    return jnp.concatenate(
        [moved[: rows - 8], jnp.where(place < 8 - k, moved[rows - 8 :], fill)], axis=0
    )


def one_minus_exp(x, exp_neg):
    series = jnp.ones_like(x)
    for k in range(9, 1, -1):
        series = 1.0 - (x * (1.0 / k)) * series
    return jnp.where(x < 0.5, x * series, 1.0 - exp_neg)


def windows(decay, shift, levels_ref, total_ref, lanes):
    rows = decay.shape[0]
    k, level = 1, 0
    while k < rows:
        levels_ref[level, :, lanes] = decay
        decay = decay * shift(decay, k, 1.0)
        k, level = k * 2, level + 1
    total_ref[:, lanes] = decay


def scanned(value, shift, levels_ref, lanes):
    rows = value.shape[0]
    k, level = 1, 0
    while k < rows:
        value = value + levels_ref[level, :, lanes] * shift(value, k, 0.0)
        k, level = k * 2, level + 1
    return value


def kernel(
    n, chunk,
    x_hbm, cam_hbm, rate_hbm, gain_hbm, obs_hbm, prec_hbm, smooth_hbm,
    smoothed_ref, loglik_ref, grad_ref,
    x_ref, cam_ref, rate_ref, gain_ref, obs_ref, prec_ref, smooth_ref,
    inject_ref, levels_ref, cum_ref, back_ref, backcum_ref, drive_ref, local_ref, uloc_ref,
    which_ref, weight_ref, own_ref, peer_ref, direct_ref, gsend_ref, gpeer_ref,
    fsrc, fbuf, usrc, ubuf, vsrc, vbuf,
    load_sem, gain_sem, obs_sem, fsend, frecv, usend, urecv, vsend, vrecv,
    psend, precv, gsend, grecv,
):
    me = lax.axis_index("tm")
    side = lax.axis_index("inner")
    rows, feats = x_ref.shape
    chans = rate_ref.shape[1]
    cams = gain_ref.shape[0]
    halves = [slice(h, h + 128) for h in range(0, chans, 128)]

    loads = [
        pltpu.make_async_copy(src, dst, load_sem.at[i])
        for i, (src, dst) in enumerate(
            [
                (rate_hbm, rate_ref), (cam_hbm, cam_ref), (x_hbm, x_ref),
                (smooth_hbm, smooth_ref), (prec_hbm, prec_ref),
            ]
        )
    ]
    gain_loads = [
        pltpu.make_async_copy(gain_hbm.at[c], gain_ref.at[c], gain_sem.at[c]) for c in range(cams)
    ]
    obs_loads = [
        pltpu.make_async_copy(obs_hbm.at[c], obs_ref.at[c], obs_sem.at[c]) for c in range(cams)
    ]
    for copy in loads[:3] + gain_loads + loads[3:] + obs_loads:
        copy.start()

    barrier = pltpu.get_barrier_semaphore()

    def greet(s, carry):
        pl.semaphore_signal(barrier, inc=1, device_id={"tm": s}, device_id_type=MESH)
        return carry

    lax.fori_loop(0, me, greet, 0)
    lax.fori_loop(me + 1, n, greet, 0)
    pl.semaphore_signal(barrier, inc=1, device_id={"inner": 1 - side}, device_id_type=MESH)

    def message(src, buf, send, recv, s):
        return pltpu.make_async_remote_copy(
            src_ref=src, dst_ref=buf.at[me], send_sem=send.at[s], recv_sem=recv.at[me],
            device_id={"tm": s}, device_id_type=MESH,
        )

    def arrival(src, buf, send, recv, s):
        return pltpu.make_async_remote_copy(
            src_ref=src, dst_ref=buf.at[s], send_sem=send.at[s], recv_sem=recv.at[s],
            device_id={"tm": s}, device_id_type=MESH,
        )

    loads[0].wait()
    for lanes in halves:
        rate = rate_ref[:, lanes]
        decay = jnp.exp(-rate)
        inject_ref[:, lanes] = jnp.sqrt(one_minus_exp(2.0 * rate, decay * decay))
        windows(decay, down, levels_ref, cum_ref, lanes)
    loads[1].wait()
    which_ref[...] = jnp.broadcast_to(cam_ref[...].astype(F32), (128, rows)).T

    loads[2].wait()
    x = x_ref[...]
    for c in range(cams):
        gain_loads[c].wait()
        part = lax.dot_general(x, gain_ref[c], NT, preferred_element_type=F32)
        for lanes in halves:
            chosen = jnp.where(which_ref[...] == float(c), part[:, lanes], 0.0)
            if c == 0:
                drive_ref[:, lanes] = chosen
            elif c < cams - 1:
                drive_ref[:, lanes] += chosen
            else:
                drive_ref[:, lanes] = inject_ref[:, lanes] * (drive_ref[:, lanes] + chosen)

    for lanes in halves:
        local = scanned(drive_ref[:, lanes], down, levels_ref, lanes)
        local_ref[:, lanes] = local
        fsrc[0:1, lanes] = cum_ref[rows - 1 : rows, lanes]
        fsrc[1:2, lanes] = local[rows - 1 : rows]
    pl.semaphore_wait(barrier, n)

    def send_f(s, carry):
        message(fsrc, fbuf, fsend, frecv, s).start()
        return carry

    lax.fori_loop(me + 1, n, send_f, 0)

    loads[3].wait()
    for lanes in halves:
        value = drive_ref[:, lanes]
        power = smooth_ref[:, lanes]
        k = 1
        while k < rows:
            value = value + power * up(value, k, 0.0)
            power = power * power
            k *= 2
        uloc_ref[:, lanes] = value
        usrc[0:1, lanes] = value[0:1]

    def send_u(s, carry):
        message(usrc, ubuf, usend, urecv, s).start()
        return carry

    lax.fori_loop(0, me, send_u, 0)

    for lanes in halves:
        drive_ref[:, lanes] = levels_ref[0, :, lanes] * down(local_ref[:, lanes], 1, 0.0)
        windows(levels_ref[0, :, lanes], up, back_ref, backcum_ref, lanes)
    loads[4].wait()
    for lane in range(0, feats, 128):
        lanes = slice(lane, lane + 128)
        weight = jnp.broadcast_to(prec_ref[0:1, lanes], (rows, 128))
        for c in range(1, cams):
            weight = jnp.where(which_ref[...] == float(c), prec_ref[c : c + 1, lanes], weight)
        weight_ref[:, lanes] = weight

    def enter(s, carry):
        arrival(fsrc, fbuf, fsend, frecv, s).wait_recv()
        return fbuf[s, 0:1, :] * carry + fbuf[s, 1:2, :]

    entering = lax.fori_loop(0, me, enter, jnp.zeros((1, chans), F32))

    which = jnp.concatenate([which_ref[...]] * (chans // 128), axis=1)
    masks = [which == float(c) for c in range(cams)]
    predicted = drive_ref[...] + cum_ref[...] * entering
    states = [jnp.where(masks[c], predicted, 0.0).astype(BF16) for c in range(cams)]
    chunks = feats // chunk
    partials = []
    for j in range(chunks):
        total = None
        for c in range(cams):
            if j == 0:
                obs_loads[c].wait()
            part = lax.dot_general(
                states[c], obs_ref[c, j * chunk : (j + 1) * chunk, :], NT,
                preferred_element_type=F32,
            )
            total = part if total is None else total + part
        own_ref[j] = total
        copy = pltpu.make_async_remote_copy(
            src_ref=own_ref.at[j], dst_ref=peer_ref.at[j], send_sem=psend.at[j],
            recv_sem=precv.at[j], device_id={"inner": 1 - side}, device_id_type=MESH,
        )
        copy.start()
        partials.append(copy)

    edge = lax.broadcasted_iota(jnp.int32, (8, chans), 0)
    gain = smooth_ref[...]
    eight = jnp.ones((8, chans), F32)
    power = gain
    for bit in (1, 2, 4, 8):
        eight = jnp.where(((8 - edge) & bit) != 0, eight * power, eight)
        power = power * power
    step = eight[0:1]
    whole = step
    for _ in range(rows // 8 - 1):
        whole = whole * step

    def leave(i, carry):
        s = n - 1 - i
        arrival(usrc, ubuf, usend, urecv, s).wait_recv()
        return whole * carry + ubuf[s]

    leaving = lax.fori_loop(0, n - 1 - me, leave, jnp.zeros((1, chans), F32))
    smoothed_ref[...] = (
        local_ref[...] + cum_ref[...] * entering + gain * up(uloc_ref[...], 1, 0.0)
    )
    tail = eight * leaving
    for i in range(rows // 8 - 1, -1, -1):
        smoothed_ref[i * 8 : i * 8 + 8, :] += tail
        tail = tail * step

    square = jnp.zeros((rows, 128), F32)
    pull = None
    for j in range(chunks):
        partials[j].wait_recv()
        cols = slice(j * chunk, (j + 1) * chunk)
        surprise = x_ref[:, cols].astype(F32) - (own_ref[j] + peer_ref[j])
        weighted = weight_ref[:, cols] * surprise
        direct_ref[:, cols] = weighted
        terms = weighted * surprise
        for lane in range(0, chunk, 128):
            square = square + terms[:, lane : lane + 128]
        wide = jnp.concatenate([which_ref[...]] * (chunk // 128), axis=1)
        for c in range(cams):
            part = lax.dot_general(
                jnp.where(wide == float(c), weighted, 0.0).astype(BF16), obs_ref[c, cols, :], NN,
                preferred_element_type=F32,
            )
            pull = part if pull is None else pull + part

    for lanes in halves:
        back = scanned(levels_ref[0, :, lanes] * pull[:, lanes], up, back_ref, lanes)
        uloc_ref[:, lanes] = back
        vsrc[0:1, lanes] = backcum_ref[0:1, lanes]
        vsrc[1:2, lanes] = back[0:1]

    def send_v(s, carry):
        message(vsrc, vbuf, vsend, vrecv, s).start()
        return carry

    lax.fori_loop(0, me, send_v, 0)

    loglik_ref[...] = (-0.5 / feats) * jnp.sum(square.T, axis=0, keepdims=True)
    fixed = inject_ref[...] * up(uloc_ref[...], 1, 0.0)
    slope = inject_ref[...] * up(backcum_ref[...], 1, 1.0)

    def comes(i, carry):
        s = n - 1 - i
        arrival(vsrc, vbuf, vsend, vrecv, s).wait_recv()
        return vbuf[s, 0:1, :] * carry + vbuf[s, 1:2, :]

    coming = lax.fori_loop(0, n - 1 - me, comes, jnp.zeros((1, chans), F32))
    scaled = fixed + slope * coming
    states = [jnp.where(masks[c], scaled, 0.0).astype(BF16) for c in range(cams)]

    half = feats // 2

    def gradient(first):
        total = None
        cols = pl.ds(pl.multiple_of(first, 128), half)
        for c in range(cams):
            part = lax.dot_general(
                states[c], gain_ref[c, :, cols], NN, preferred_element_type=F32
            )
            total = part if total is None else total + part
        return total

    gsend_ref[...] = gradient((1 - side) * half)
    shared = pltpu.make_async_remote_copy(
        src_ref=gsend_ref, dst_ref=gpeer_ref, send_sem=gsend, recv_sem=grecv,
        device_id={"inner": 1 - side}, device_id_type=MESH,
    )
    shared.start()
    mine = pl.multiple_of(side * half, 128)
    grad_ref[...] = gradient(side * half) - direct_ref[:, pl.ds(mine, half)]
    shared.wait_recv()
    grad_ref[...] += gpeer_ref[...]

    def sent_f(s, carry):
        message(fsrc, fbuf, fsend, frecv, s).wait_send()
        return carry

    def sent_back(s, carry):
        message(usrc, ubuf, usend, urecv, s).wait_send()
        message(vsrc, vbuf, vsend, vrecv, s).wait_send()
        return carry

    lax.fori_loop(me + 1, n, sent_f, 0)
    lax.fori_loop(0, me, sent_back, 0)
    for copy in partials:
        copy.wait_send()
    shared.wait_send()


def on_device(
    n, x, camera, decay_rate, kalman_gain, operator, precision, smooth_gain
):
    rows, feats = x.shape
    chans = decay_rate.shape[1]
    cams = kalman_gain.shape[0]
    chunk = 256
    chunks = feats // chunk
    steps = (rows - 1).bit_length()
    vm = pltpu.VMEM
    dma = pltpu.SemaphoreType.DMA
    state = (rows, chans)
    smoothed, loglik, grad = pl.pallas_call(
        functools.partial(kernel, n, chunk),
        out_shape=(
            jax.ShapeDtypeStruct((rows, chans), F32),
            jax.ShapeDtypeStruct((1, rows), F32),
            jax.ShapeDtypeStruct((rows, feats // 2), F32),
        ),
        in_specs=[pl.BlockSpec(memory_space=pltpu.HBM)] * 7,
        out_specs=(pl.BlockSpec(memory_space=pltpu.VMEM),) * 3,
        scratch_shapes=[
            vm((rows, feats), BF16), vm((1, rows), jnp.int32), vm(state, F32),
            vm((cams, chans, feats), BF16), vm((cams, feats, chans), BF16),
            vm((cams, feats), F32), vm((1, chans), F32),
            vm(state, F32), vm((steps, rows, chans), F32), vm(state, F32),
            vm((steps, rows, chans), F32), vm(state, F32), vm(state, F32), vm(state, F32),
            vm(state, F32),
            vm((rows, 128), F32), vm((rows, feats), F32),
            vm((chunks, rows, chunk), F32), vm((chunks, rows, chunk), F32),
            vm((rows, feats), F32), vm((rows, feats // 2), F32), vm((rows, feats // 2), F32),
            vm((2, chans), F32), vm((n, 2, chans), F32),
            vm((1, chans), F32), vm((n, 1, chans), F32),
            vm((2, chans), F32), vm((n, 2, chans), F32),
            dma((5,)), dma((cams,)), dma((cams,)),
            dma((n,)), dma((n,)), dma((n,)), dma((n,)), dma((n,)), dma((n,)),
            dma((chunks,)), dma((chunks,)), dma, dma,
        ],
        compiler_params=pltpu.CompilerParams(
            collective_id=0, has_side_effects=True, vmem_limit_bytes=63 * 1024 * 1024
        ),
    )(
        x, camera.reshape(1, rows), decay_rate, kalman_gain, operator, precision,
        smooth_gain.reshape(1, chans),
    )
    return smoothed, loglik.reshape(rows), grad


def solution(mesh):
    placed = (
        P(("groups", "tm"), None),
        P(("groups", "tm")),
        P(("groups", "tm"), "inner"),
        P(None, "inner", None),
        P(None, None, "inner"),
        P(),
        P(("groups", "inner")),
    )
    return jax.shard_map(
        functools.partial(on_device, mesh.shape["tm"]),
        mesh=mesh,
        in_specs=placed,
        out_specs=(P(("groups", "tm"), "inner"), P(("groups", "tm")), P(("groups", "tm"), "inner")),
        check_vma=False,
    )
```

```python
import functools

import jax
import jax.numpy as jnp
from jax import lax
from jax.experimental import pallas as pl
from jax.experimental.pallas import tpu as pltpu
from jax.sharding import PartitionSpec as P

MESH = pl.DeviceIdType.MESH
F32 = jnp.float32
BF16 = jnp.bfloat16
NT = (((1,), (1,)), ((), ()))
NN = (((1,), (0,)), ((), ()))


def down(x, k, fill):
    rows = x.shape[0]
    if k % 8 == 0:
        return jnp.concatenate([jnp.full((k, x.shape[1]), fill, x.dtype), x[: rows - k]], axis=0)
    moved = pltpu.roll(x, k, 0)
    place = lax.broadcasted_iota(jnp.int32, (8, x.shape[1]), 0)
    return jnp.concatenate([jnp.where(place >= k, moved[:8], fill), moved[8:]], axis=0)


def up(x, k, fill):
    rows = x.shape[0]
    if k % 8 == 0:
        return jnp.concatenate([x[k:], jnp.full((k, x.shape[1]), fill, x.dtype)], axis=0)
    moved = pltpu.roll(x, rows - k, 0)
    place = lax.broadcasted_iota(jnp.int32, (8, x.shape[1]), 0)
    return jnp.concatenate(
        [moved[: rows - 8], jnp.where(place < 8 - k, moved[rows - 8 :], fill)], axis=0
    )


def one_minus_exp(x, exp_neg):
    series = jnp.ones_like(x)
    for k in range(9, 1, -1):
        series = 1.0 - (x * (1.0 / k)) * series
    return jnp.where(x < 0.5, x * series, 1.0 - exp_neg)


def windows(decay, shift, levels_ref, total_ref, lanes):
    rows = decay.shape[0]
    k, level = 1, 0
    while k < rows:
        levels_ref[level, :, lanes] = decay
        decay = decay * shift(decay, k, 1.0)
        k, level = k * 2, level + 1
    total_ref[:, lanes] = decay


def scanned(value, shift, levels_ref, lanes):
    rows = value.shape[0]
    k, level = 1, 0
    while k < rows:
        value = value + levels_ref[level, :, lanes] * shift(value, k, 0.0)
        k, level = k * 2, level + 1
    return value


def kernel(
    n, chunk,
    x_hbm, cam_hbm, rate_hbm, gain_hbm, obs_hbm, prec_hbm, smooth_hbm,
    smoothed_ref, loglik_ref, grad_ref,
    x_ref, cam_ref, rate_ref, gain_ref, obs_ref, prec_ref, smooth_ref,
    inject_ref, levels_ref, cum_ref, back_ref, backcum_ref, drive_ref, local_ref, uloc_ref,
    which_ref, weight_ref, own_ref, peer_ref, direct_ref, gsend_ref, gpeer_ref,
    fsrc, fbuf, usrc, ubuf, vsrc, vbuf,
    load_sem, gain_sem, obs_sem, fsend, frecv, usend, urecv, vsend, vrecv,
    psend, precv, gsend, grecv,
):
    me = lax.axis_index("tm")
    side = lax.axis_index("inner")
    rows, feats = x_ref.shape
    chans = rate_ref.shape[1]
    cams = gain_ref.shape[0]
    halves = [slice(h, h + 128) for h in range(0, chans, 128)]

    loads = [
        pltpu.make_async_copy(src, dst, load_sem.at[i])
        for i, (src, dst) in enumerate(
            [
                (rate_hbm, rate_ref), (cam_hbm, cam_ref), (x_hbm, x_ref),
                (smooth_hbm, smooth_ref), (prec_hbm, prec_ref),
            ]
        )
    ]
    gain_loads = [
        pltpu.make_async_copy(gain_hbm.at[c], gain_ref.at[c], gain_sem.at[c]) for c in range(cams)
    ]
    obs_loads = [
        pltpu.make_async_copy(obs_hbm.at[c], obs_ref.at[c], obs_sem.at[c]) for c in range(cams)
    ]
    for copy in loads[:3] + gain_loads + loads[3:] + obs_loads:
        copy.start()

    barrier = pltpu.get_barrier_semaphore()

    def greet(s, carry):
        pl.semaphore_signal(barrier, inc=1, device_id={"tm": s}, device_id_type=MESH)
        return carry

    lax.fori_loop(0, me, greet, 0)
    lax.fori_loop(me + 1, n, greet, 0)
    pl.semaphore_signal(barrier, inc=1, device_id={"inner": 1 - side}, device_id_type=MESH)

    def message(src, buf, send, recv, s):
        return pltpu.make_async_remote_copy(
            src_ref=src, dst_ref=buf.at[me], send_sem=send.at[s], recv_sem=recv.at[me],
            device_id={"tm": s}, device_id_type=MESH,
        )

    def arrival(src, buf, send, recv, s):
        return pltpu.make_async_remote_copy(
            src_ref=src, dst_ref=buf.at[s], send_sem=send.at[s], recv_sem=recv.at[s],
            device_id={"tm": s}, device_id_type=MESH,
        )

    loads[0].wait()
    for lanes in halves:
        rate = rate_ref[:, lanes]
        decay = jnp.exp(-rate)
        inject_ref[:, lanes] = jnp.sqrt(one_minus_exp(2.0 * rate, decay * decay))
        windows(decay, down, levels_ref, cum_ref, lanes)
    loads[1].wait()
    which_ref[...] = jnp.broadcast_to(cam_ref[...].astype(F32), (128, rows)).T

    loads[2].wait()
    x = x_ref[...]
    for c in range(cams):
        gain_loads[c].wait()
        part = lax.dot_general(x, gain_ref[c], NT, preferred_element_type=F32)
        for lanes in halves:
            chosen = jnp.where(which_ref[...] == float(c), part[:, lanes], 0.0)
            if c == 0:
                drive_ref[:, lanes] = chosen
            elif c < cams - 1:
                drive_ref[:, lanes] += chosen
            else:
                drive_ref[:, lanes] = inject_ref[:, lanes] * (drive_ref[:, lanes] + chosen)

    for lanes in halves:
        local = scanned(drive_ref[:, lanes], down, levels_ref, lanes)
        local_ref[:, lanes] = local
        fsrc[0:1, lanes] = cum_ref[rows - 1 : rows, lanes]
        fsrc[1:2, lanes] = local[rows - 1 : rows]
    pl.semaphore_wait(barrier, n)

    def send_f(s, carry):
        message(fsrc, fbuf, fsend, frecv, s).start()
        return carry

    lax.fori_loop(me + 1, n, send_f, 0)

    loads[3].wait()
    for lanes in halves:
        value = drive_ref[:, lanes]
        power = smooth_ref[:, lanes]
        k = 1
        while k < rows:
            value = value + power * up(value, k, 0.0)
            power = power * power
            k *= 2
        uloc_ref[:, lanes] = value
        usrc[0:1, lanes] = value[0:1]

    def send_u(s, carry):
        message(usrc, ubuf, usend, urecv, s).start()
        return carry

    lax.fori_loop(0, me, send_u, 0)

    for lanes in halves:
        drive_ref[:, lanes] = levels_ref[0, :, lanes] * down(local_ref[:, lanes], 1, 0.0)
        windows(levels_ref[0, :, lanes], up, back_ref, backcum_ref, lanes)
    loads[4].wait()
    for lane in range(0, feats, 128):
        lanes = slice(lane, lane + 128)
        weight = jnp.broadcast_to(prec_ref[0:1, lanes], (rows, 128))
        for c in range(1, cams):
            weight = jnp.where(which_ref[...] == float(c), prec_ref[c : c + 1, lanes], weight)
        weight_ref[:, lanes] = weight

    def enter(s, carry):
        arrival(fsrc, fbuf, fsend, frecv, s).wait_recv()
        return fbuf[s, 0:1, :] * carry + fbuf[s, 1:2, :]

    entering = lax.fori_loop(0, me, enter, jnp.zeros((1, chans), F32))

    which = jnp.concatenate([which_ref[...]] * (chans // 128), axis=1)
    masks = [which == float(c) for c in range(cams)]
    predicted = drive_ref[...] + cum_ref[...] * entering
    states = [jnp.where(masks[c], predicted, 0.0).astype(BF16) for c in range(cams)]
    chunks = feats // chunk
    partials = []
    for j in range(chunks):
        total = None
        for c in range(cams):
            if j == 0:
                obs_loads[c].wait()
            part = lax.dot_general(
                states[c], obs_ref[c, j * chunk : (j + 1) * chunk, :], NT,
                preferred_element_type=F32,
            )
            total = part if total is None else total + part
        own_ref[j] = total
        copy = pltpu.make_async_remote_copy(
            src_ref=own_ref.at[j], dst_ref=peer_ref.at[j], send_sem=psend.at[j],
            recv_sem=precv.at[j], device_id={"inner": 1 - side}, device_id_type=MESH,
        )
        copy.start()
        partials.append(copy)

    edge = lax.broadcasted_iota(jnp.int32, (8, chans), 0)
    gain = smooth_ref[...]
    eight = jnp.ones((8, chans), F32)
    power = gain
    for bit in (1, 2, 4, 8):
        eight = jnp.where(((8 - edge) & bit) != 0, eight * power, eight)
        power = power * power
    step = eight[0:1]
    whole = step
    for _ in range(rows // 8 - 1):
        whole = whole * step

    def leave(i, carry):
        s = n - 1 - i
        arrival(usrc, ubuf, usend, urecv, s).wait_recv()
        return whole * carry + ubuf[s]

    leaving = lax.fori_loop(0, n - 1 - me, leave, jnp.zeros((1, chans), F32))
    smoothed_ref[...] = (
        local_ref[...] + cum_ref[...] * entering + gain * up(uloc_ref[...], 1, 0.0)
    )
    tail = eight * leaving
    for i in range(rows // 8 - 1, -1, -1):
        smoothed_ref[i * 8 : i * 8 + 8, :] += tail
        tail = tail * step

    square = jnp.zeros((rows, 128), F32)
    pull = None
    for j in range(chunks):
        partials[j].wait_recv()
        cols = slice(j * chunk, (j + 1) * chunk)
        surprise = x_ref[:, cols].astype(F32) - (own_ref[j] + peer_ref[j])
        weighted = weight_ref[:, cols] * surprise
        direct_ref[:, cols] = weighted
        terms = weighted * surprise
        for lane in range(0, chunk, 128):
            square = square + terms[:, lane : lane + 128]
        wide = jnp.concatenate([which_ref[...]] * (chunk // 128), axis=1)
        for c in range(cams):
            part = lax.dot_general(
                jnp.where(wide == float(c), weighted, 0.0).astype(BF16), obs_ref[c, cols, :], NN,
                preferred_element_type=F32,
            )
            pull = part if pull is None else pull + part

    for lanes in halves:
        back = scanned(levels_ref[0, :, lanes] * pull[:, lanes], up, back_ref, lanes)
        uloc_ref[:, lanes] = back
        vsrc[0:1, lanes] = backcum_ref[0:1, lanes]
        vsrc[1:2, lanes] = back[0:1]

    def send_v(s, carry):
        message(vsrc, vbuf, vsend, vrecv, s).start()
        return carry

    lax.fori_loop(0, me, send_v, 0)

    loglik_ref[...] = (-0.5 / feats) * jnp.sum(square.T, axis=0, keepdims=True)
    fixed = inject_ref[...] * up(uloc_ref[...], 1, 0.0)
    slope = inject_ref[...] * up(backcum_ref[...], 1, 1.0)

    def comes(i, carry):
        s = n - 1 - i
        arrival(vsrc, vbuf, vsend, vrecv, s).wait_recv()
        return vbuf[s, 0:1, :] * carry + vbuf[s, 1:2, :]

    coming = lax.fori_loop(0, n - 1 - me, comes, jnp.zeros((1, chans), F32))
    scaled = fixed + slope * coming
    states = [jnp.where(masks[c], scaled, 0.0).astype(BF16) for c in range(cams)]

    half = feats // 2

    def gradient(first):
        total = None
        cols = pl.ds(pl.multiple_of(first, 128), half)
        for c in range(cams):
            part = lax.dot_general(
                states[c], gain_ref[c, :, cols], NN, preferred_element_type=F32
            )
            total = part if total is None else total + part
        return total

    gsend_ref[...] = gradient((1 - side) * half)
    shared = pltpu.make_async_remote_copy(
        src_ref=gsend_ref, dst_ref=gpeer_ref, send_sem=gsend, recv_sem=grecv,
        device_id={"inner": 1 - side}, device_id_type=MESH,
    )
    shared.start()
    mine = pl.multiple_of(side * half, 128)
    grad_ref[...] = gradient(side * half) - direct_ref[:, pl.ds(mine, half)]
    shared.wait_recv()
    grad_ref[...] += gpeer_ref[...]

    def sent_f(s, carry):
        message(fsrc, fbuf, fsend, frecv, s).wait_send()
        return carry

    def sent_back(s, carry):
        message(usrc, ubuf, usend, urecv, s).wait_send()
        message(vsrc, vbuf, vsend, vrecv, s).wait_send()
        return carry

    lax.fori_loop(me + 1, n, sent_f, 0)
    lax.fori_loop(0, me, sent_back, 0)
    for copy in partials:
        copy.wait_send()
    shared.wait_send()


def on_device(
    n, x, camera, decay_rate, kalman_gain, operator, precision, smooth_gain
):
    rows, feats = x.shape
    chans = decay_rate.shape[1]
    cams = kalman_gain.shape[0]
    chunk = 256
    chunks = feats // chunk
    steps = (rows - 1).bit_length()
    vm = pltpu.VMEM
    dma = pltpu.SemaphoreType.DMA
    state = (rows, chans)
    smoothed, loglik, grad = pl.pallas_call(
        functools.partial(kernel, n, chunk),
        out_shape=(
            jax.ShapeDtypeStruct((rows, chans), F32),
            jax.ShapeDtypeStruct((1, rows), F32),
            jax.ShapeDtypeStruct((rows, feats // 2), F32),
        ),
        in_specs=[pl.BlockSpec(memory_space=pltpu.HBM)] * 7,
        out_specs=(pl.BlockSpec(memory_space=pltpu.VMEM),) * 3,
        scratch_shapes=[
            vm((rows, feats), BF16), vm((1, rows), jnp.int32), vm(state, F32),
            vm((cams, chans, feats), BF16), vm((cams, feats, chans), BF16),
            vm((cams, feats), F32), vm((1, chans), F32),
            vm(state, F32), vm((steps, rows, chans), F32), vm(state, F32),
            vm((steps, rows, chans), F32), vm(state, F32), vm(state, F32), vm(state, F32),
            vm(state, F32),
            vm((rows, 128), F32), vm((rows, feats), F32),
            vm((chunks, rows, chunk), F32), vm((chunks, rows, chunk), F32),
            vm((rows, feats), F32), vm((rows, feats // 2), F32), vm((rows, feats // 2), F32),
            vm((2, chans), F32), vm((n, 2, chans), F32),
            vm((1, chans), F32), vm((n, 1, chans), F32),
            vm((2, chans), F32), vm((n, 2, chans), F32),
            dma((5,)), dma((cams,)), dma((cams,)),
            dma((n,)), dma((n,)), dma((n,)), dma((n,)), dma((n,)), dma((n,)),
            dma((chunks,)), dma((chunks,)), dma, dma,
        ],
        compiler_params=pltpu.CompilerParams(
            collective_id=0, has_side_effects=True, vmem_limit_bytes=40 * 1024 * 1024
        ),
    )(
        *(
            pltpu.with_memory_space_constraint(array, pltpu.HBM)
            for array in (
                x, camera.reshape(1, rows), decay_rate, kalman_gain, operator, precision,
                smooth_gain.reshape(1, chans),
            )
        )
    )
    return smoothed, loglik.reshape(rows), grad


def solution(mesh):
    placed = (
        P(("groups", "tm"), None),
        P(("groups", "tm")),
        P(("groups", "tm"), "inner"),
        P(None, "inner", None),
        P(None, None, "inner"),
        P(),
        P(("groups", "inner")),
    )
    return jax.shard_map(
        functools.partial(on_device, mesh.shape["tm"]),
        mesh=mesh,
        in_specs=placed,
        out_specs=(P(("groups", "tm"), "inner"), P(("groups", "tm")), P(("groups", "tm"), "inner")),
        check_vma=False,
    )
```

```python
import functools

import jax
import jax.numpy as jnp
from jax import lax
from jax.experimental import pallas as pl
from jax.experimental.pallas import tpu as pltpu
from jax.sharding import PartitionSpec as P

MESH = pl.DeviceIdType.MESH
F32 = jnp.float32
BF16 = jnp.bfloat16
NT = (((1,), (1,)), ((), ()))
NN = (((1,), (0,)), ((), ()))


def down(x, k, fill):
    rows = x.shape[0]
    if k % 8 == 0:
        return jnp.concatenate([jnp.full((k, x.shape[1]), fill, x.dtype), x[: rows - k]], axis=0)
    moved = pltpu.roll(x, k, 0)
    place = lax.broadcasted_iota(jnp.int32, (8, x.shape[1]), 0)
    return jnp.concatenate([jnp.where(place >= k, moved[:8], fill), moved[8:]], axis=0)


def up(x, k, fill):
    rows = x.shape[0]
    if k % 8 == 0:
        return jnp.concatenate([x[k:], jnp.full((k, x.shape[1]), fill, x.dtype)], axis=0)
    moved = pltpu.roll(x, rows - k, 0)
    place = lax.broadcasted_iota(jnp.int32, (8, x.shape[1]), 0)
    return jnp.concatenate(
        [moved[: rows - 8], jnp.where(place < 8 - k, moved[rows - 8 :], fill)], axis=0
    )


def one_minus_exp(x, exp_neg):
    series = jnp.ones_like(x)
    for k in range(9, 1, -1):
        series = 1.0 - (x * (1.0 / k)) * series
    return jnp.where(x < 0.5, x * series, 1.0 - exp_neg)


def windows(decay, shift, levels_ref, total_ref, lanes):
    rows = decay.shape[0]
    k, level = 1, 0
    while k < rows:
        levels_ref[level, :, lanes] = decay
        decay = decay * shift(decay, k, 1.0)
        k, level = k * 2, level + 1
    total_ref[:, lanes] = decay


def scanned(value, shift, levels_ref, lanes):
    rows = value.shape[0]
    k, level = 1, 0
    while k < rows:
        value = value + levels_ref[level, :, lanes] * shift(value, k, 0.0)
        k, level = k * 2, level + 1
    return value


def kernel(
    n, chunk,
    x_hbm, cam_hbm, rate_hbm, gain_hbm, obs_hbm, prec_hbm, smooth_hbm,
    smoothed_ref, loglik_ref, grad_ref,
    x_ref, cam_ref, rate_ref, gain_ref, obs_ref, flip_ref, prec_ref, smooth_ref,
    inject_ref, levels_ref, cum_ref, back_ref, backcum_ref, drive_ref, local_ref, uloc_ref,
    which_ref, weight_ref, own_ref, peer_ref, direct_ref, gsend_ref, gpeer_ref,
    fsrc, fbuf, usrc, ubuf, vsrc, vbuf,
    load_sem, gain_sem, obs_sem, fsend, frecv, usend, urecv, vsend, vrecv,
    psend, precv, gsend, grecv,
):
    me = lax.axis_index("tm")
    side = lax.axis_index("inner")
    rows, feats = x_ref.shape
    chans = rate_ref.shape[1]
    cams = gain_ref.shape[0]
    halves = [slice(h, h + 128) for h in range(0, chans, 128)]

    barrier = pltpu.get_barrier_semaphore()

    def greet(s, carry):
        pl.semaphore_signal(barrier, inc=1, device_id={"tm": s}, device_id_type=MESH)
        return carry

    lax.fori_loop(0, me, greet, 0)
    lax.fori_loop(0, n - 1 - me, lambda i, carry: greet(n - 1 - i, carry), 0)
    pl.semaphore_signal(barrier, inc=1, device_id={"inner": 1 - side}, device_id_type=MESH)

    loads = [
        pltpu.make_async_copy(src, dst, load_sem.at[i])
        for i, (src, dst) in enumerate(
            [
                (rate_hbm, rate_ref), (cam_hbm, cam_ref), (x_hbm, x_ref),
                (smooth_hbm, smooth_ref), (prec_hbm, prec_ref),
            ]
        )
    ]
    gain_loads = [
        pltpu.make_async_copy(gain_hbm.at[c], gain_ref.at[c], gain_sem.at[c]) for c in range(cams)
    ]
    obs_loads = [
        pltpu.make_async_copy(obs_hbm.at[c], obs_ref.at[c], obs_sem.at[c]) for c in range(cams)
    ]
    for copy in loads[:3] + gain_loads + loads[3:] + obs_loads:
        copy.start()

    def message(src, buf, send, recv, s):
        return pltpu.make_async_remote_copy(
            src_ref=src, dst_ref=buf.at[me], send_sem=send.at[s], recv_sem=recv.at[me],
            device_id={"tm": s}, device_id_type=MESH,
        )

    def arrival(src, buf, send, recv, s):
        return pltpu.make_async_remote_copy(
            src_ref=src, dst_ref=buf.at[s], send_sem=send.at[s], recv_sem=recv.at[s],
            device_id={"tm": s}, device_id_type=MESH,
        )

    loads[0].wait()
    for lanes in halves:
        rate = rate_ref[:, lanes]
        decay = jnp.exp(-rate)
        inject_ref[:, lanes] = jnp.sqrt(one_minus_exp(2.0 * rate, decay * decay))
        windows(decay, down, levels_ref, cum_ref, lanes)
    loads[1].wait()
    which_ref[...] = jnp.broadcast_to(cam_ref[...].astype(F32), (128, rows)).T

    loads[2].wait()
    x = x_ref[...]
    for c in range(cams):
        gain_loads[c].wait()
        part = lax.dot_general(x, gain_ref[c], NT, preferred_element_type=F32)
        for lanes in halves:
            chosen = jnp.where(which_ref[...] == float(c), part[:, lanes], 0.0)
            if c == 0:
                drive_ref[:, lanes] = chosen
            elif c < cams - 1:
                drive_ref[:, lanes] += chosen
            else:
                drive_ref[:, lanes] = inject_ref[:, lanes] * (drive_ref[:, lanes] + chosen)

    for lanes in halves:
        local = scanned(drive_ref[:, lanes], down, levels_ref, lanes)
        local_ref[:, lanes] = local
        fsrc[0:1, lanes] = cum_ref[rows - 1 : rows, lanes]
        fsrc[1:2, lanes] = local[rows - 1 : rows]
    pl.semaphore_wait(barrier, n)

    def send_f(i, carry):
        message(fsrc, fbuf, fsend, frecv, n - 1 - i).start()
        return carry

    lax.fori_loop(0, n - 1 - me, send_f, 0)

    loads[3].wait()
    for lanes in halves:
        value = drive_ref[:, lanes]
        power = smooth_ref[:, lanes]
        k = 1
        while k < rows:
            value = value + power * up(value, k, 0.0)
            power = power * power
            k *= 2
        uloc_ref[:, lanes] = value
        usrc[0:1, lanes] = value[0:1]

    def send_u(s, carry):
        message(usrc, ubuf, usend, urecv, s).start()
        return carry

    lax.fori_loop(0, me, send_u, 0)

    for lanes in halves:
        drive_ref[:, lanes] = levels_ref[0, :, lanes] * down(local_ref[:, lanes], 1, 0.0)
        windows(levels_ref[0, :, lanes], up, back_ref, backcum_ref, lanes)
    loads[4].wait()
    for lane in range(0, feats, 128):
        lanes = slice(lane, lane + 128)
        weight = jnp.broadcast_to(prec_ref[0:1, lanes], (rows, 128))
        for c in range(1, cams):
            weight = jnp.where(which_ref[...] == float(c), prec_ref[c : c + 1, lanes], weight)
        weight_ref[:, lanes] = weight

    for c in range(cams):
        obs_loads[c].wait()
        flip_ref[c] = obs_ref[c].T

    def enter(s, carry):
        arrival(fsrc, fbuf, fsend, frecv, s).wait_recv()
        return fbuf[s, 0:1, :] * carry + fbuf[s, 1:2, :]

    entering = lax.fori_loop(0, me, enter, jnp.zeros((1, chans), F32))

    which = jnp.concatenate([which_ref[...]] * (chans // 128), axis=1)
    masks = [which == float(c) for c in range(cams)]
    predicted = drive_ref[...] + cum_ref[...] * entering
    states = [jnp.where(masks[c], predicted, 0.0).astype(BF16) for c in range(cams)]
    chunks = feats // chunk
    partials = []
    for j in range(chunks):
        total = None
        for c in range(cams):
            part = lax.dot_general(
                states[c], flip_ref[c, :, j * chunk : (j + 1) * chunk], NN,
                preferred_element_type=F32,
            )
            total = part if total is None else total + part
        own_ref[j] = total
        copy = pltpu.make_async_remote_copy(
            src_ref=own_ref.at[j], dst_ref=peer_ref.at[j], send_sem=psend.at[j],
            recv_sem=precv.at[j], device_id={"inner": 1 - side}, device_id_type=MESH,
        )
        copy.start()
        partials.append(copy)

    edge = lax.broadcasted_iota(jnp.int32, (8, chans), 0)
    gain = smooth_ref[...]
    eight = jnp.ones((8, chans), F32)
    power = gain
    for bit in (1, 2, 4, 8):
        eight = jnp.where(((8 - edge) & bit) != 0, eight * power, eight)
        power = power * power
    step = eight[0:1]
    whole = step
    for _ in range(rows // 8 - 1):
        whole = whole * step

    def leave(i, carry):
        s = n - 1 - i
        arrival(usrc, ubuf, usend, urecv, s).wait_recv()
        return whole * carry + ubuf[s]

    leaving = lax.fori_loop(0, n - 1 - me, leave, jnp.zeros((1, chans), F32))
    smoothed_ref[...] = (
        local_ref[...] + cum_ref[...] * entering + gain * up(uloc_ref[...], 1, 0.0)
    )
    tail = eight * leaving
    for i in range(rows // 8 - 1, -1, -1):
        smoothed_ref[i * 8 : i * 8 + 8, :] += tail
        tail = tail * step

    square = jnp.zeros((rows, 128), F32)
    pull = None
    for j in range(chunks):
        partials[j].wait_recv()
        cols = slice(j * chunk, (j + 1) * chunk)
        surprise = x_ref[:, cols].astype(F32) - (own_ref[j] + peer_ref[j])
        weighted = weight_ref[:, cols] * surprise
        direct_ref[:, cols] = weighted
        terms = weighted * surprise
        for lane in range(0, chunk, 128):
            square = square + terms[:, lane : lane + 128]
        wide = jnp.concatenate([which_ref[...]] * (chunk // 128), axis=1)
        for c in range(cams):
            part = lax.dot_general(
                jnp.where(wide == float(c), weighted, 0.0).astype(BF16), obs_ref[c, cols, :], NN,
                preferred_element_type=F32,
            )
            pull = part if pull is None else pull + part

    for lanes in halves:
        back = scanned(levels_ref[0, :, lanes] * pull[:, lanes], up, back_ref, lanes)
        uloc_ref[:, lanes] = back
        vsrc[0:1, lanes] = backcum_ref[0:1, lanes]
        vsrc[1:2, lanes] = back[0:1]

    def send_v(s, carry):
        message(vsrc, vbuf, vsend, vrecv, s).start()
        return carry

    lax.fori_loop(0, me, send_v, 0)

    loglik_ref[...] = (-0.5 / feats) * jnp.sum(square.T, axis=0, keepdims=True)
    fixed = inject_ref[...] * up(uloc_ref[...], 1, 0.0)
    slope = inject_ref[...] * up(backcum_ref[...], 1, 1.0)

    def comes(i, carry):
        s = n - 1 - i
        arrival(vsrc, vbuf, vsend, vrecv, s).wait_recv()
        return vbuf[s, 0:1, :] * carry + vbuf[s, 1:2, :]

    coming = lax.fori_loop(0, n - 1 - me, comes, jnp.zeros((1, chans), F32))
    scaled = fixed + slope * coming
    states = [jnp.where(masks[c], scaled, 0.0).astype(BF16) for c in range(cams)]

    half = feats // 2

    def gradient(first):
        total = None
        cols = pl.ds(pl.multiple_of(first, 128), half)
        for c in range(cams):
            part = lax.dot_general(
                states[c], gain_ref[c, :, cols], NN, preferred_element_type=F32
            )
            total = part if total is None else total + part
        return total

    gsend_ref[...] = gradient((1 - side) * half)
    shared = pltpu.make_async_remote_copy(
        src_ref=gsend_ref, dst_ref=gpeer_ref, send_sem=gsend, recv_sem=grecv,
        device_id={"inner": 1 - side}, device_id_type=MESH,
    )
    shared.start()
    mine = pl.multiple_of(side * half, 128)
    grad_ref[...] = gradient(side * half) - direct_ref[:, pl.ds(mine, half)]
    shared.wait_recv()
    grad_ref[...] += gpeer_ref[...]

    def sent_f(s, carry):
        message(fsrc, fbuf, fsend, frecv, s).wait_send()
        return carry

    def sent_back(s, carry):
        message(usrc, ubuf, usend, urecv, s).wait_send()
        message(vsrc, vbuf, vsend, vrecv, s).wait_send()
        return carry

    lax.fori_loop(me + 1, n, sent_f, 0)
    lax.fori_loop(0, me, sent_back, 0)
    for copy in partials:
        copy.wait_send()
    shared.wait_send()


def leave_vmem(smoothed, loglik, grad, smoothed_out, loglik_out, grad_out, sem):
    copies = [
        pltpu.make_async_copy(src, dst, sem.at[i])
        for i, (src, dst) in enumerate(
            [(grad, grad_out), (smoothed, smoothed_out), (loglik, loglik_out)]
        )
    ]
    for copy in copies:
        copy.start()
    for copy in copies:
        copy.wait()


def on_device(
    n, x, camera, decay_rate, kalman_gain, operator, precision, smooth_gain
):
    rows, feats = x.shape
    chans = decay_rate.shape[1]
    cams = kalman_gain.shape[0]
    chunk = 256
    chunks = feats // chunk
    steps = (rows - 1).bit_length()
    vm = pltpu.VMEM
    dma = pltpu.SemaphoreType.DMA
    state = (rows, chans)
    smoothed, loglik, grad = pl.pallas_call(
        functools.partial(kernel, n, chunk),
        out_shape=(
            jax.ShapeDtypeStruct((rows, chans), F32),
            jax.ShapeDtypeStruct((1, rows), F32),
            jax.ShapeDtypeStruct((rows, feats // 2), F32),
        ),
        in_specs=[pl.BlockSpec(memory_space=pltpu.HBM)] * 7,
        out_specs=(pl.BlockSpec(memory_space=pltpu.VMEM),) * 3,
        scratch_shapes=[
            vm((rows, feats), BF16), vm((1, rows), jnp.int32), vm(state, F32),
            vm((cams, chans, feats), BF16), vm((cams, feats, chans), BF16),
            vm((cams, chans, feats), BF16),
            vm((cams, feats), F32), vm((1, chans), F32),
            vm(state, F32), vm((steps, rows, chans), F32), vm(state, F32),
            vm((steps, rows, chans), F32), vm(state, F32), vm(state, F32), vm(state, F32),
            vm(state, F32),
            vm((rows, 128), F32), vm((rows, feats), F32),
            vm((chunks, rows, chunk), F32), vm((chunks, rows, chunk), F32),
            vm((rows, feats), F32), vm((rows, feats // 2), F32), vm((rows, feats // 2), F32),
            vm((2, chans), F32), vm((n, 2, chans), F32),
            vm((1, chans), F32), vm((n, 1, chans), F32),
            vm((2, chans), F32), vm((n, 2, chans), F32),
            dma((5,)), dma((cams,)), dma((cams,)),
            dma((n,)), dma((n,)), dma((n,)), dma((n,)), dma((n,)), dma((n,)),
            dma((chunks,)), dma((chunks,)), dma, dma,
        ],
        compiler_params=pltpu.CompilerParams(
            collective_id=0, has_side_effects=True, vmem_limit_bytes=40 * 1024 * 1024
        ),
    )(
        *(
            pltpu.with_memory_space_constraint(array, pltpu.HBM)
            for array in (
                x, camera.reshape(1, rows), decay_rate, kalman_gain, operator, precision,
                smooth_gain.reshape(1, chans),
            )
        )
    )
    smoothed, loglik, grad = pl.pallas_call(
        leave_vmem,
        out_shape=tuple(jax.ShapeDtypeStruct(a.shape, a.dtype) for a in (smoothed, loglik, grad)),
        in_specs=[pl.BlockSpec(memory_space=pltpu.VMEM)] * 3,
        out_specs=(pl.BlockSpec(memory_space=pltpu.HBM),) * 3,
        scratch_shapes=[dma((3,))],
    )(*(pltpu.with_memory_space_constraint(a, pltpu.VMEM) for a in (smoothed, loglik, grad)))
    return smoothed, loglik.reshape(rows), grad


def solution(mesh):
    placed = (
        P(("groups", "tm"), None),
        P(("groups", "tm")),
        P(("groups", "tm"), "inner"),
        P(None, "inner", None),
        P(None, None, "inner"),
        P(),
        P(("groups", "inner")),
    )
    return jax.shard_map(
        functools.partial(on_device, mesh.shape["tm"]),
        mesh=mesh,
        in_specs=placed,
        out_specs=(P(("groups", "tm"), "inner"), P(("groups", "tm")), P(("groups", "tm"), "inner")),
        check_vma=False,
    )
```

```python
import functools

import jax
import jax.numpy as jnp
from jax import lax
from jax.experimental import pallas as pl
from jax.experimental.pallas import tpu as pltpu
from jax.sharding import PartitionSpec as P

MESH = pl.DeviceIdType.MESH
F32 = jnp.float32
BF16 = jnp.bfloat16
NT = (((1,), (1,)), ((), ()))
NN = (((1,), (0,)), ((), ()))


def down(x, k, fill):
    rows = x.shape[0]
    if k % 8 == 0:
        return jnp.concatenate([jnp.full((k, x.shape[1]), fill, x.dtype), x[: rows - k]], axis=0)
    moved = pltpu.roll(x, k, 0)
    place = lax.broadcasted_iota(jnp.int32, (8, x.shape[1]), 0)
    return jnp.concatenate([jnp.where(place >= k, moved[:8], fill), moved[8:]], axis=0)


def up(x, k, fill):
    rows = x.shape[0]
    if k % 8 == 0:
        return jnp.concatenate([x[k:], jnp.full((k, x.shape[1]), fill, x.dtype)], axis=0)
    moved = pltpu.roll(x, rows - k, 0)
    place = lax.broadcasted_iota(jnp.int32, (8, x.shape[1]), 0)
    return jnp.concatenate(
        [moved[: rows - 8], jnp.where(place < 8 - k, moved[rows - 8 :], fill)], axis=0
    )


def one_minus_exp(x, exp_neg):
    series = jnp.ones_like(x)
    for k in range(9, 1, -1):
        series = 1.0 - (x * (1.0 / k)) * series
    return jnp.where(x < 0.5, x * series, 1.0 - exp_neg)


def windows(decay, shift, levels_ref, total_ref, lanes):
    rows = decay.shape[0]
    k, level = 1, 0
    while k < rows:
        levels_ref[level, :, lanes] = decay
        decay = decay * shift(decay, k, 1.0)
        k, level = k * 2, level + 1
    total_ref[:, lanes] = decay


def scanned(value, shift, levels_ref, lanes):
    rows = value.shape[0]
    k, level = 1, 0
    while k < rows:
        value = value + levels_ref[level, :, lanes] * shift(value, k, 0.0)
        k, level = k * 2, level + 1
    return value


def kernel(
    n, chunk,
    x_hbm, cam_hbm, rate_hbm, gain_hbm, obs_hbm, prec_hbm, smooth_hbm,
    smoothed_ref, loglik_ref, grad_ref,
    x_ref, cam_ref, rate_ref, gain_ref, obs_ref, flip_ref, prec_ref, smooth_ref,
    inject_ref, levels_ref, cum_ref, back_ref, backcum_ref, drive_ref, local_ref, uloc_ref,
    which_ref, weight_ref, own_ref, peer_ref, direct_ref, state_ref, speer_ref,
    ksend_ref, kpeer_ref, kept_ref, wbuf,
    fsrc, fbuf, usrc, ubuf, vsrc, vbuf,
    load_sem, gain_sem, obs_sem, fsend, frecv, usend, urecv, vsend, vrecv,
    psend, precv, gsend, grecv, ksend, krecv, wsend, wrecv,
):
    me = lax.axis_index("tm")
    side = lax.axis_index("inner")
    rows, feats = x_ref.shape
    chans = rate_ref.shape[1]
    cams = gain_ref.shape[0]
    halves = [slice(h, h + 128) for h in range(0, chans, 128)]

    barrier = pltpu.get_barrier_semaphore()

    def greet(s, carry):
        for core in (side, 1 - side):
            pl.semaphore_signal(
                barrier, inc=1, device_id={"tm": s, "inner": core}, device_id_type=MESH
            )
        return carry

    lax.fori_loop(0, me, greet, 0)
    lax.fori_loop(0, n - 1 - me, lambda i, carry: greet(n - 1 - i, carry), 0)
    pl.semaphore_signal(barrier, inc=1, device_id={"inner": 1 - side}, device_id_type=MESH)

    loads = [
        pltpu.make_async_copy(src, dst, load_sem.at[i])
        for i, (src, dst) in enumerate(
            [
                (rate_hbm, rate_ref), (cam_hbm, cam_ref), (x_hbm, x_ref),
                (smooth_hbm, smooth_ref), (prec_hbm, prec_ref),
            ]
        )
    ]
    gain_loads = [
        pltpu.make_async_copy(gain_hbm.at[c], gain_ref.at[c], gain_sem.at[c]) for c in range(cams)
    ]
    obs_loads = [
        pltpu.make_async_copy(obs_hbm.at[c], obs_ref.at[c], obs_sem.at[c]) for c in range(cams)
    ]
    for copy in loads[:3] + gain_loads + loads[3:] + obs_loads:
        copy.start()

    def message(src, buf, send, recv, s):
        return pltpu.make_async_remote_copy(
            src_ref=src, dst_ref=buf.at[me], send_sem=send.at[s], recv_sem=recv.at[me],
            device_id={"tm": s}, device_id_type=MESH,
        )

    def across(s):
        return pltpu.make_async_remote_copy(
            src_ref=vsrc, dst_ref=wbuf.at[me], send_sem=wsend.at[s], recv_sem=wrecv.at[me],
            device_id={"tm": s, "inner": 1 - side}, device_id_type=MESH,
        )

    def arrival(src, buf, send, recv, s):
        return pltpu.make_async_remote_copy(
            src_ref=src, dst_ref=buf.at[s], send_sem=send.at[s], recv_sem=recv.at[s],
            device_id={"tm": s}, device_id_type=MESH,
        )

    loads[0].wait()
    for lanes in halves:
        rate = rate_ref[:, lanes]
        decay = jnp.exp(-rate)
        inject_ref[:, lanes] = jnp.sqrt(one_minus_exp(2.0 * rate, decay * decay))
        windows(decay, down, levels_ref, cum_ref, lanes)
    loads[1].wait()
    which_ref[...] = jnp.broadcast_to(cam_ref[...].astype(F32), (128, rows)).T

    loads[2].wait()
    x = x_ref[...]
    for c in range(cams):
        gain_loads[c].wait()
        part = lax.dot_general(x, gain_ref[c], NT, preferred_element_type=F32)
        for lanes in halves:
            chosen = jnp.where(which_ref[...] == float(c), part[:, lanes], 0.0)
            if c == 0:
                drive_ref[:, lanes] = chosen
            elif c < cams - 1:
                drive_ref[:, lanes] += chosen
            else:
                drive_ref[:, lanes] = inject_ref[:, lanes] * (drive_ref[:, lanes] + chosen)

    for lanes in halves:
        local = scanned(drive_ref[:, lanes], down, levels_ref, lanes)
        local_ref[:, lanes] = local
        fsrc[0:1, lanes] = cum_ref[rows - 1 : rows, lanes]
        fsrc[1:2, lanes] = local[rows - 1 : rows]
    pl.semaphore_wait(barrier, 2 * n - 1)

    def send_f(i, carry):
        message(fsrc, fbuf, fsend, frecv, n - 1 - i).start()
        return carry

    lax.fori_loop(0, n - 1 - me, send_f, 0)

    loads[3].wait()
    for lanes in halves:
        value = drive_ref[:, lanes]
        power = smooth_ref[:, lanes]
        k = 1
        while k < rows:
            value = value + power * up(value, k, 0.0)
            power = power * power
            k *= 2
        uloc_ref[:, lanes] = value
        usrc[0:1, lanes] = value[0:1]

    def send_u(s, carry):
        message(usrc, ubuf, usend, urecv, s).start()
        return carry

    lax.fori_loop(0, me, send_u, 0)

    half = feats // 2
    mine = pl.multiple_of(side * half, 128)
    others = pl.ds(pl.multiple_of((1 - side) * half, 128), half)
    gains = []
    for c in range(cams):
        ksend_ref[c] = gain_ref[c, :, others].astype(F32)
        copy = pltpu.make_async_remote_copy(
            src_ref=ksend_ref.at[c], dst_ref=kpeer_ref.at[c], send_sem=ksend.at[c],
            recv_sem=krecv.at[c], device_id={"inner": 1 - side}, device_id_type=MESH,
        )
        copy.start()
        gains.append(copy)

    for lanes in halves:
        drive_ref[:, lanes] = levels_ref[0, :, lanes] * down(local_ref[:, lanes], 1, 0.0)
        windows(levels_ref[0, :, lanes], up, back_ref, backcum_ref, lanes)
    loads[4].wait()
    for lane in range(0, feats, 128):
        lanes = slice(lane, lane + 128)
        weight = jnp.broadcast_to(prec_ref[0:1, lanes], (rows, 128))
        for c in range(1, cams):
            weight = jnp.where(which_ref[...] == float(c), prec_ref[c : c + 1, lanes], weight)
        weight_ref[:, lanes] = weight

    for c in range(cams):
        obs_loads[c].wait()
        flip_ref[c] = obs_ref[c].T

    def enter(s, carry):
        arrival(fsrc, fbuf, fsend, frecv, s).wait_recv()
        return fbuf[s, 0:1, :] * carry + fbuf[s, 1:2, :]

    entering = lax.fori_loop(0, me, enter, jnp.zeros((1, chans), F32))

    which = jnp.concatenate([which_ref[...]] * (chans // 128), axis=1)
    masks = [which == float(c) for c in range(cams)]
    predicted = drive_ref[...] + cum_ref[...] * entering
    states = [jnp.where(masks[c], predicted, 0.0).astype(BF16) for c in range(cams)]
    chunks = feats // chunk
    partials = []
    for j in range(chunks):
        total = None
        for c in range(cams):
            part = lax.dot_general(
                states[c], flip_ref[c, :, j * chunk : (j + 1) * chunk], NN,
                preferred_element_type=F32,
            )
            total = part if total is None else total + part
        own_ref[j] = total
        copy = pltpu.make_async_remote_copy(
            src_ref=own_ref.at[j], dst_ref=peer_ref.at[j], send_sem=psend.at[j],
            recv_sem=precv.at[j], device_id={"inner": 1 - side}, device_id_type=MESH,
        )
        copy.start()
        partials.append(copy)

    edge = lax.broadcasted_iota(jnp.int32, (8, chans), 0)
    gain = smooth_ref[...]
    eight = jnp.ones((8, chans), F32)
    power = gain
    for bit in (1, 2, 4, 8):
        eight = jnp.where(((8 - edge) & bit) != 0, eight * power, eight)
        power = power * power
    step = eight[0:1]
    whole = step
    for _ in range(rows // 8 - 1):
        whole = whole * step

    def leave(i, carry):
        s = n - 1 - i
        arrival(usrc, ubuf, usend, urecv, s).wait_recv()
        return whole * carry + ubuf[s]

    leaving = lax.fori_loop(0, n - 1 - me, leave, jnp.zeros((1, chans), F32))
    smoothed_ref[...] = (
        local_ref[...] + cum_ref[...] * entering + gain * up(uloc_ref[...], 1, 0.0)
    )
    tail = eight * leaving
    for i in range(rows // 8 - 1, -1, -1):
        smoothed_ref[i * 8 : i * 8 + 8, :] += tail
        tail = tail * step

    square = jnp.zeros((rows, 128), F32)
    pull = None
    for j in range(chunks):
        partials[j].wait_recv()
        cols = slice(j * chunk, (j + 1) * chunk)
        surprise = x_ref[:, cols].astype(F32) - (own_ref[j] + peer_ref[j])
        weighted = weight_ref[:, cols] * surprise
        direct_ref[:, cols] = weighted
        terms = weighted * surprise
        for lane in range(0, chunk, 128):
            square = square + terms[:, lane : lane + 128]
        wide = jnp.concatenate([which_ref[...]] * (chunk // 128), axis=1)
        for c in range(cams):
            part = lax.dot_general(
                jnp.where(wide == float(c), weighted, 0.0).astype(BF16), obs_ref[c, cols, :], NN,
                preferred_element_type=F32,
            )
            pull = part if pull is None else pull + part

    for lanes in halves:
        back = scanned(levels_ref[0, :, lanes] * pull[:, lanes], up, back_ref, lanes)
        uloc_ref[:, lanes] = back
        vsrc[0:1, lanes] = backcum_ref[0:1, lanes]
        vsrc[1:2, lanes] = back[0:1]

    def send_v(s, carry):
        message(vsrc, vbuf, vsend, vrecv, s).start()
        across(s).start()
        return carry

    lax.fori_loop(0, me, send_v, 0)

    state_ref[0] = inject_ref[...] * up(uloc_ref[...], 1, 0.0)
    state_ref[1] = inject_ref[...] * up(backcum_ref[...], 1, 1.0)
    shared = pltpu.make_async_remote_copy(
        src_ref=state_ref, dst_ref=speer_ref, send_sem=gsend, recv_sem=grecv,
        device_id={"inner": 1 - side}, device_id_type=MESH,
    )
    shared.start()
    loglik_ref[...] = (-0.5 / feats) * jnp.sum(square.T, axis=0, keepdims=True)
    for c in range(cams):
        gains[c].wait_recv()
        kept_ref[c] = kpeer_ref[c].astype(BF16)
    shared.wait_recv()

    def comes(i, carry):
        s = n - 1 - i
        arrival(vsrc, vbuf, vsend, vrecv, s).wait_recv()
        arrival(vsrc, wbuf, wsend, wrecv, s).wait_recv()
        return (
            vbuf[s, 0:1, :] * carry[0] + vbuf[s, 1:2, :],
            wbuf[s, 0:1, :] * carry[1] + wbuf[s, 1:2, :],
        )

    nothing = jnp.zeros((1, chans), F32)
    coming = lax.fori_loop(0, n - 1 - me, comes, (nothing, nothing))
    scaled = state_ref[0] + state_ref[1] * coming[0]
    theirs = speer_ref[0] + speer_ref[1] * coming[1]
    total = None
    for c in range(cams):
        part = lax.dot_general(
            jnp.where(masks[c], scaled, 0.0).astype(BF16), gain_ref[c, :, pl.ds(mine, half)], NN,
            preferred_element_type=F32,
        ) + lax.dot_general(
            jnp.where(masks[c], theirs, 0.0).astype(BF16), kept_ref[c], NN,
            preferred_element_type=F32,
        )
        total = part if total is None else total + part
    grad_ref[...] = total - direct_ref[:, pl.ds(mine, half)]

    def sent_f(s, carry):
        message(fsrc, fbuf, fsend, frecv, s).wait_send()
        return carry

    def sent_back(s, carry):
        message(usrc, ubuf, usend, urecv, s).wait_send()
        message(vsrc, vbuf, vsend, vrecv, s).wait_send()
        across(s).wait_send()
        return carry

    lax.fori_loop(me + 1, n, sent_f, 0)
    lax.fori_loop(0, me, sent_back, 0)
    for copy in partials + gains:
        copy.wait_send()
    shared.wait_send()


def leave_vmem(smoothed, loglik, grad, smoothed_out, loglik_out, grad_out, sem):
    copies = [
        pltpu.make_async_copy(src, dst, sem.at[i])
        for i, (src, dst) in enumerate(
            [(grad, grad_out), (smoothed, smoothed_out), (loglik, loglik_out)]
        )
    ]
    for copy in copies:
        copy.start()
    for copy in copies:
        copy.wait()


def on_device(
    n, x, camera, decay_rate, kalman_gain, operator, precision, smooth_gain
):
    rows, feats = x.shape
    chans = decay_rate.shape[1]
    cams = kalman_gain.shape[0]
    chunk = 256
    chunks = feats // chunk
    steps = (rows - 1).bit_length()
    vm = pltpu.VMEM
    dma = pltpu.SemaphoreType.DMA
    state = (rows, chans)
    smoothed, loglik, grad = pl.pallas_call(
        functools.partial(kernel, n, chunk),
        out_shape=(
            jax.ShapeDtypeStruct((rows, chans), F32),
            jax.ShapeDtypeStruct((1, rows), F32),
            jax.ShapeDtypeStruct((rows, feats // 2), F32),
        ),
        in_specs=[pl.BlockSpec(memory_space=pltpu.HBM)] * 7,
        out_specs=(pl.BlockSpec(memory_space=pltpu.VMEM),) * 3,
        scratch_shapes=[
            vm((rows, feats), BF16), vm((1, rows), jnp.int32), vm(state, F32),
            vm((cams, chans, feats), BF16), vm((cams, feats, chans), BF16),
            vm((cams, chans, feats), BF16),
            vm((cams, feats), F32), vm((1, chans), F32),
            vm(state, F32), vm((steps, rows, chans), F32), vm(state, F32),
            vm((steps, rows, chans), F32), vm(state, F32), vm(state, F32), vm(state, F32),
            vm(state, F32),
            vm((rows, 128), F32), vm((rows, feats), F32),
            vm((chunks, rows, chunk), F32), vm((chunks, rows, chunk), F32),
            vm((rows, feats), F32), vm((2, rows, chans), F32),
            vm((2, rows, chans), F32), vm((cams, chans, feats // 2), F32),
            vm((cams, chans, feats // 2), F32), vm((cams, chans, feats // 2), BF16),
            vm((n, 2, chans), F32),
            vm((2, chans), F32), vm((n, 2, chans), F32),
            vm((1, chans), F32), vm((n, 1, chans), F32),
            vm((2, chans), F32), vm((n, 2, chans), F32),
            dma((5,)), dma((cams,)), dma((cams,)),
            dma((n,)), dma((n,)), dma((n,)), dma((n,)), dma((n,)), dma((n,)),
            dma((chunks,)), dma((chunks,)), dma, dma,
            dma((cams,)), dma((cams,)), dma((n,)), dma((n,)),
        ],
        compiler_params=pltpu.CompilerParams(
            collective_id=0, has_side_effects=True, vmem_limit_bytes=40 * 1024 * 1024
        ),
    )(
        *(
            pltpu.with_memory_space_constraint(array, pltpu.HBM)
            for array in (
                x, camera.reshape(1, rows), decay_rate, kalman_gain, operator, precision,
                smooth_gain.reshape(1, chans),
            )
        )
    )
    smoothed, loglik, grad = pl.pallas_call(
        leave_vmem,
        out_shape=tuple(jax.ShapeDtypeStruct(a.shape, a.dtype) for a in (smoothed, loglik, grad)),
        in_specs=[pl.BlockSpec(memory_space=pltpu.VMEM)] * 3,
        out_specs=(pl.BlockSpec(memory_space=pltpu.HBM),) * 3,
        scratch_shapes=[dma((3,))],
    )(*(pltpu.with_memory_space_constraint(a, pltpu.VMEM) for a in (smoothed, loglik, grad)))
    return smoothed, loglik.reshape(rows), grad


def solution(mesh):
    placed = (
        P(("groups", "tm"), None),
        P(("groups", "tm")),
        P(("groups", "tm"), "inner"),
        P(None, "inner", None),
        P(None, None, "inner"),
        P(),
        P(("groups", "inner")),
    )
    return jax.shard_map(
        functools.partial(on_device, mesh.shape["tm"]),
        mesh=mesh,
        in_specs=placed,
        out_specs=(P(("groups", "tm"), "inner"), P(("groups", "tm")), P(("groups", "tm"), "inner")),
        check_vma=False,
    )
```
